256 devices in a mesh: cluster: 16 (over x, y), sub: 16 (over z, core).
Axes of the slice: x: 4, y: 4, z: 8, core: 2. Of those that a mesh axis runs over, the one named last changes fastest.
Arguments:
- dual_ops: float32 [16, 16, 1408, 1408], P('cluster', 'sub'), may hold values from -1 to 4.5, as said below
- contributions: float32 [16, 16, 1408, 64], P('cluster', 'sub'), may hold values from -6 to 6
- block_sizes: int32 [16, 16, 4], P('cluster', 'sub'), may hold values from 0 to 352, as said below
- mult_map: int32 [16, 16, 1408], P('cluster', 'sub'), may hold values from 0 to 1407, each once within a row
- coarse_basis: float32 [16, 16, 32, 704], P('cluster', 'sub'), may hold values from -0.21875 to 0.21875
- coarse_inverse: float32 [16, 512, 512], P('cluster'), may hold values from -0.1 to 0.5, as said below
Outputs:
- solution: float32 [16, 16, 1408, 64], P('cluster', 'sub')
- residual: float32 [16, 16, 1408, 64], P('cluster', 'sub')
The draws below stay inside these ranges and needn't reach their ends.
Inputs may be any that keep to these rules, and one draw needn't show every extreme that they name: `dual_ops`: symmetric positive definite for each subdomain. block_sizes[c, s, k] equals the count on the facing side of the neighbour across side k; sides at the ends of an axis hold 0, all others 352 // 4 to 352; some side holds exactly 352. `mult_map`: for each subdomain a permutation of the 1408 slots. `coarse_inverse`: symmetric for each cluster.
All inputs are finite; a program needn't handle non-finite values.
Results may differ from the reference program's by a relative error of at most 0.0003.
Values sent between devices are 32-bit elements; how exact they have to be, the bound alone decides.
A program may use at most 64 MiB of HBM per device.

```python
import math
import jax
import jax.numpy as jnp
from jax import lax

M = 1408
PAD = 352
MODES = 32
R = 64
ITERS = 2
CLUSTERS = 16
SUBS = 16
COARSE = 512


def one_operator(subkey):
    first_key, second_key = jax.random.split(subkey)
    noise_matrix = jax.random.normal(first_key, (M, M), jnp.float32)
    diagonal_values = jnp.exp(jax.random.uniform(second_key, (M,), jnp.float32, math.log(1.2), math.log(3.6)))
    return (noise_matrix + noise_matrix.T) * (1.0 / (2.8 * math.sqrt(M))) + jnp.diag(diagonal_values)


def draw_dual_ops(key, part):
    subkeys = jax.random.split(jax.random.fold_in(key, 7), CLUSTERS * SUBS)
    return lax.map(one_operator, subkeys).reshape(CLUSTERS, SUBS, M, M)


def draw_block_sizes(key, part):
    first_key, second_key = jax.random.split(jax.random.fold_in(key, 11))
    sub_edges = jax.random.randint(first_key, (CLUSTERS, SUBS - 1), PAD // 4, PAD + 1).astype(jnp.int32)
    sub_edges = sub_edges.at[0, 0].set(PAD)
    cluster_edges = jax.random.randint(second_key, (CLUSTERS - 1, SUBS), PAD // 4, PAD + 1).astype(jnp.int32)
    zero_column = jnp.zeros((CLUSTERS, 1), jnp.int32)
    zero_line = jnp.zeros((1, SUBS), jnp.int32)
    west_side = jnp.concatenate([zero_column, sub_edges], axis=1)
    east_side = jnp.concatenate([sub_edges, zero_column], axis=1)
    south_side = jnp.concatenate([zero_line, cluster_edges], axis=0)
    north_side = jnp.concatenate([cluster_edges, zero_line], axis=0)
    return jnp.stack([west_side, east_side, south_side, north_side], axis=-1).astype(jnp.int32)


def draw_coarse_inverse(key, part):
    first_key, second_key = jax.random.split(jax.random.fold_in(key, 13))
    noise_matrix = jax.random.normal(first_key, (CLUSTERS, COARSE, COARSE), jnp.float32)
    diagonal_values = jnp.exp(jax.random.uniform(second_key, (CLUSTERS, COARSE), jnp.float32, math.log(0.1), math.log(0.3)))
    symmetric = (noise_matrix + jnp.swapaxes(noise_matrix, 1, 2)) * (0.002 / math.sqrt(2.0))
    return symmetric + diagonal_values[..., None] * jnp.eye(COARSE, dtype=jnp.float32)[None]


def level_of(own_key, dims, cuts, smallest, largest):
    def one(position, parts):
        draws = jax.random.uniform(jax.random.fold_in(jax.random.fold_in(own_key, 6), position), (parts,), jnp.float32, smallest / len(cuts), largest / len(cuts))
        return jnp.repeat(jnp.exp(draws), dims[position] // parts).reshape((-1,) + (1,) * (len(dims) - position - 1))

    level = one(*cuts[0])
    for cut in cuts[1:]:
        level = level * one(*cut)
    return level


def normal_values(stream_key, dims, scale, most, cuts=(), kind=jnp.bfloat16):
    level = level_of(stream_key, dims, cuts, -0.22, 0.18) if cuts else 1.0
    entries = jax.random.normal(stream_key, dims, jnp.float32) * scale * level
    return jnp.minimum(jnp.maximum(entries, -most), most).astype(kind)


def setup_inputs(seed: int = 0) -> dict:
    keys = jax.random.split(jax.random.key(seed), 7)
    dual_ops = draw_dual_ops(jax.random.fold_in(keys[6], 71), 0)
    contributions = normal_values(keys[1], (CLUSTERS, SUBS, M, R), 1.0, 6.0, ((0, 16), (1, 16)), jnp.float32)
    block_sizes = draw_block_sizes(jax.random.fold_in(keys[6], 71), 0)
    mult_map = jax.vmap(lambda own: jax.random.permutation(own, M))(jax.random.split(keys[3], CLUSTERS * SUBS)).reshape((CLUSTERS, SUBS, M)).astype(jnp.int32)
    coarse_basis = normal_values(keys[4], (CLUSTERS, SUBS, MODES, 2 * PAD), (2 * PAD) ** -0.5, 0.21875, ((0, 16), (1, 16)), jnp.float32)
    coarse_inverse = draw_coarse_inverse(jax.random.fold_in(keys[6], 71), 0)
    return dict(dual_ops=dual_ops, contributions=contributions, block_sizes=block_sizes, mult_map=mult_map, coarse_basis=coarse_basis, coarse_inverse=coarse_inverse)


precise = lax.Precision.HIGHEST

def slot_weights(block_sizes):
    row_index = jnp.arange(M, dtype=jnp.int32)
    row_side = row_index // PAD
    row_place = row_index % PAD
    side_match = row_side[None, None, :, None] == jnp.arange(4, dtype=jnp.int32)[None, None, None, :]
    row_limit = jnp.sum(jnp.where(side_match, block_sizes[:, :, None, :], 0), axis=3)
    live_rows = (row_place[None, None, :] < row_limit).astype(jnp.float32)[..., None]
    row_sign = jnp.where(row_side % 2 == 0, -1.0, 1.0).astype(jnp.float32)
    return (live_rows, live_rows * row_sign[None, None, :, None])

def assemble(values, live_rows, row_weight):
    blocks = (values * row_weight).reshape(CLUSTERS, SUBS, 4, PAD, R)
    west_part = blocks[:, :, 0]
    east_part = blocks[:, :, 1]
    south_part = blocks[:, :, 2]
    north_part = blocks[:, :, 3]
    zero_sub = jnp.zeros((CLUSTERS, 1, PAD, R), jnp.float32)
    zero_cluster = jnp.zeros((1, SUBS, PAD, R), jnp.float32)
    new_west = west_part + jnp.concatenate([zero_sub, east_part[:, :-1]], axis=1)
    new_east = east_part + jnp.concatenate([west_part[:, 1:], zero_sub], axis=1)
    new_south = south_part + jnp.concatenate([zero_cluster, north_part[:-1]], axis=0)
    new_north = north_part + jnp.concatenate([south_part[1:], zero_cluster], axis=0)
    joined = jnp.stack([new_west, new_east, new_south, new_north], axis=2)
    return joined.reshape(CLUSTERS, SUBS, M, R) * live_rows

def apply_dual(values, dual_ops, mult_map, inverse_map, live_rows, row_weight):
    local_vals = jnp.take_along_axis(values * row_weight, mult_map[..., None], axis=2)
    mapped = jnp.einsum('csmn,csnr->csmr', dual_ops, local_vals, precision=precise)
    return assemble(jnp.take_along_axis(mapped, inverse_map[..., None], axis=2), live_rows, row_weight)

def project(values, coarse_basis, coarse_inverse, live_rows, row_weight):
    signed = (values * row_weight)[:, :, :2 * PAD]
    moments = jnp.einsum('cskp,cspr->cskr', coarse_basis, signed, precision=precise).reshape(CLUSTERS, COARSE, R)
    coefficients = jnp.einsum('cij,cjr->cir', coarse_inverse, moments, precision=precise).reshape(CLUSTERS, SUBS, MODES, R)
    lifted = jnp.einsum('cskp,cskr->cspr', coarse_basis, coefficients, precision=precise)
    padded = jnp.concatenate([lifted, jnp.zeros((CLUSTERS, SUBS, 2 * PAD, R), jnp.float32)], axis=2)
    return values - assemble(padded, live_rows, row_weight)

def inner_product(left, right):
    return 0.5 * jnp.einsum('csmi,csmj->ij', left, right, precision=precise)

def chol_solve(factor, target):
    middle = lax.linalg.triangular_solve(factor, target, left_side=True, lower=True)
    return lax.linalg.triangular_solve(factor, middle, left_side=True, lower=True, transpose_a=True)

def times_small(vectors, small):
    return jnp.einsum('csmi,ij->csmj', vectors, small, precision=precise)

def reference(dual_ops, contributions, block_sizes, mult_map, coarse_basis, coarse_inverse):
    live_rows, row_weight = slot_weights(block_sizes)
    inverse_map = jnp.argsort(mult_map, axis=-1).astype(jnp.int32)

    def projected(values):
        return project(values, coarse_basis, coarse_inverse, live_rows, row_weight)
    residual = projected(assemble(contributions, live_rows, row_weight))
    solution = jnp.zeros_like(residual)
    direction = residual
    for iteration in range(ITERS):
        mapped = projected(apply_dual(projected(direction), dual_ops, mult_map, inverse_map, live_rows, row_weight))
        curvature = inner_product(direction, mapped)
        descent = inner_product(direction, residual)
        factor = jnp.linalg.cholesky(curvature)
        step_size = chol_solve(factor, descent)
        solution = solution + times_small(direction, step_size)
        residual = residual - times_small(mapped, step_size)
        if iteration + 1 < ITERS:
            coupling = inner_product(mapped, residual)
            direction_mix = -chol_solve(factor, coupling)
            direction = residual + times_small(direction, direction_mix)
    return (solution, residual)
```

```python
import jax
import jax.numpy as jnp
from jax import lax
from jax.sharding import PartitionSpec as P
from jax.experimental import pallas as pl
from jax.experimental.pallas import tpu as pltpu


ROWS = 1408
FACE = 352
SIDE = 384
WIDE = 4 * SIDE
PAIR = 2 * SIDE
COLS = 64
MODES = 32
SUBS = 16
COARSE = 512
SIGNS = (-1.0, 1.0, -1.0, 1.0)
FACING = (1, 0, 3, 2)

F32 = jnp.float32
BF16 = jnp.bfloat16
NN = (((1,), (0,)), ((), ()))
NT = (((1,), (1,)), ((), ()))


def exact(left, right, dims=NN):
    return lax.dot_general(
        left, right, dims, precision=lax.Precision.HIGHEST, preferred_element_type=F32
    )


def single(left, right):
    return lax.dot_general(left, right, NN, preferred_element_type=F32)


def split(value):
    high = value.astype(BF16)
    return high, (value - high.astype(F32)).astype(BF16)


def fold(value):
    half = value.shape[0] // 2
    return jnp.concatenate([value[:half], value[half:]], axis=1)


def unfold(value):
    half = value.shape[1] // 2
    return jnp.concatenate([value[:, :half], value[:, half:]], axis=0)


def part(side):
    return slice(side * SIDE, (side + 1) * SIDE)


def kernel(
    ops_hbm, contrib_hbm, sizes, map_ref, basis_hbm, coarse_hbm,
    sol_hbm, res_hbm,
    full, high, low, scatter, gather,
    own_rhs, halo_rhs, own_basis, near_basis, coarse, moments_map,
    weights, first, dirs, resid, proj, image, image_proj, local,
    halo_one, halo_two, near_one, near_two, out_one, out_two, far_one, far_two,
    all_q, all_m, all_one, all_two, mixed, table_even, table_odd, dense_m,
    sum_a, sum_b, sum_c, square, out_sol, out_res,
    local_sem, send_sem, recv_sem,
):
    c, s = lax.axis_index("cluster"), lax.axis_index("sub")
    x, y = lax.div(c, 4), lax.rem(c, 4)
    z, core = lax.div(s, 2), lax.rem(s, 2)
    down, up = lax.rem(s + SUBS - 1, SUBS), lax.rem(s + 1, SUBS)
    west, east = lax.rem(c + 15, 16), lax.rem(c + 1, 16)
    mate = z * 2 + 1 - core
    x_peers = [(lax.rem(x + i, 4) * 4 + y, s) for i in range(1, 4)]
    y_peers = [(x * 4 + lax.rem(y + i, 4), s) for i in range(1, 4)]
    z_peers = [(c, lax.rem(z + i, 8) * 2 + core) for i in range(1, 8)]
    side_peers = ((c, down), (c, up), (west, s), (east, s))
    used = [0]

    def fresh():
        used[0] += 1
        return used[0] - 1

    loads = [
        pltpu.make_async_copy(contrib_hbm.at[0, 0], own_rhs, local_sem.at[0]),
        pltpu.make_async_copy(basis_hbm.at[0, 0], own_basis, local_sem.at[1]),
        pltpu.make_async_copy(
            coarse_hbm.at[0], coarse.at[pl.ds(MODES, COARSE)], local_sem.at[2]
        ),
        pltpu.make_async_copy(ops_hbm.at[0, 0], full, local_sem.at[3]),
    ]
    for load in loads:
        load.start()

    barrier = pltpu.get_barrier_semaphore()
    greeted = [(c, mate)] + z_peers + x_peers + y_peers
    greeted += [(c, down), (c, up), (west, s), (east, s)]
    for peer in greeted:
        pl.semaphore_signal(
            barrier, inc=1, device_id=peer, device_id_type=pl.DeviceIdType.MESH
        )
    pl.semaphore_wait(barrier, len(greeted))

    def send(source, target, peer, slot):
        copy = pltpu.make_async_remote_copy(
            src_ref=source, dst_ref=target,
            send_sem=send_sem.at[slot], recv_sem=recv_sem.at[slot],
            device_id=peer, device_id_type=pl.DeviceIdType.MESH,
        )
        copy.start()
        return copy

    pending = []

    def share(buffer, me, peers):
        slot = fresh()
        for peer in peers:
            send(buffer.at[me], buffer.at[me], peer, slot)
        whole = buffer.at[pl.ds(0, len(peers))]
        pending.append(lambda: pltpu.make_async_copy(whole, whole, send_sem.at[slot]).wait())
        return pltpu.make_async_copy(whole, whole, recv_sem.at[slot])

    def swap(source, target, peer):
        copy = send(source, target, peer, fresh())
        pending.append(copy.wait_send)
        return copy

    rhs_copies = [
        swap(
            contrib_hbm.at[0, 0, pl.ds(side * FACE, FACE)],
            halo_rhs.at[FACING[side]], side_peers[side],
        )
        for side in range(4)
    ]
    basis_copies = [
        swap(basis_hbm.at[0, 0], near_basis.at[1], (c, down)),
        swap(basis_hbm.at[0, 0], near_basis.at[0], (c, up)),
    ]

    slots = map_ref[0]
    slots = slots + (SIDE - FACE) * (
        (slots >= FACE).astype(jnp.int32)
        + (slots >= 2 * FACE).astype(jnp.int32)
        + (slots >= 3 * FACE).astype(jnp.int32)
    )

    def fill_scatter(step, carry):
        rows = pl.ds(pl.multiple_of(step * 128, 128), 128)
        index = lax.broadcasted_iota(jnp.int32, (128, ROWS), 0) + step * 128
        scatter[rows, :] = jnp.where(index == slots, 1.0, 0.0).astype(BF16)
        return carry

    lax.fori_loop(0, WIDE // 128, fill_scatter, 0)
    columns = lax.broadcasted_iota(jnp.int32, (128, 128), 1).astype(F32)
    for step in range(ROWS // 128):
        piece = slots[:, step * 128 : (step + 1) * 128].astype(F32)
        tall = jnp.broadcast_to(piece, (128, 128)).T
        for tile in range(WIDE // 128):
            gather[step * 128 : (step + 1) * 128, tile * 128 : (tile + 1) * 128] = (
                jnp.where(tall == columns + float(tile * 128), 1.0, 0.0).astype(BF16)
            )

    lanes = lax.broadcasted_iota(jnp.int32, (8, SIDE), 1)
    for side in range(4):
        weights[:, part(side)] = jnp.where(lanes < sizes[0, 0, side], SIGNS[side], 0.0)

    loads[1].wait()
    zero_lanes = jnp.zeros((MODES, SIDE - FACE), F32)

    def half_basis(value, side):
        return jnp.concatenate(
            [value[:, side * FACE : (side + 1) * FACE], zero_lanes], axis=1
        )

    weight_low, weight_high = weights[0:1, part(0)], weights[0:1, part(1)]
    empty = jnp.zeros((MODES, SIDE), F32)
    mine = own_basis[...]
    moments_map[MODES : 2 * MODES, part(0)] = half_basis(mine, 0) * weight_low
    moments_map[MODES : 2 * MODES, part(1)] = half_basis(mine, 1) * weight_high
    for copy in basis_copies:
        copy.wait_recv()
    moments_map[0:MODES, part(0)] = -half_basis(near_basis[0], 1) * weight_low
    moments_map[0:MODES, part(1)] = empty
    moments_map[2 * MODES : 3 * MODES, part(0)] = empty
    moments_map[2 * MODES : 3 * MODES, part(1)] = (
        -half_basis(near_basis[1], 0) * weight_high
    )
    moments_map[3 * MODES : 4 * MODES, :] = jnp.zeros((MODES, PAIR), F32)

    def gather_start(buffer, value):
        buffer[core, z] = value
        return share(buffer.at[core], z, z_peers)

    def gather_finish(buffer, arrived):
        arrived.wait()
        return swap(buffer.at[core], buffer.at[core], (c, mate))

    m_own = exact(moments_map[MODES : 2 * MODES, :], moments_map[...], NT)
    m_arrived = gather_start(all_m, m_own)

    loads[0].wait()
    for copy in rhs_copies:
        copy.wait_recv()
    index = lax.broadcasted_iota(jnp.int32, (FACE, COLS), 0)
    zero_rows = jnp.zeros((SIDE - FACE, COLS), F32)
    for side in range(4):
        own = own_rhs[side * FACE : (side + 1) * FACE, :]
        joined = jnp.where(
            index < sizes[0, 0, side], SIGNS[side] * (own - halo_rhs[side]), 0.0
        )
        first[:, part(side)] = jnp.concatenate([joined, zero_rows], axis=0).T
    q_moments = exact(moments_map[MODES : 2 * MODES, :], first[:, :PAIR], NT)
    q_arrived = gather_start(all_q, fold(q_moments))

    loads[3].wait()

    def split_rows(step, carry):
        rows = pl.ds(pl.multiple_of(step * 64, 64), 64)
        high[rows, :], low[rows, :] = split(full[rows, :])
        return carry

    loads[2].wait()
    coarse[0:MODES, :] = jnp.zeros((MODES, COARSE), F32)
    coarse[MODES + COARSE :, :] = jnp.zeros((2 * MODES, COARSE), F32)
    near_rows = coarse[pl.ds(pl.multiple_of(s * MODES, MODES), 4 * MODES), :]
    near = near_rows.T

    m_crossed = gather_finish(all_m, m_arrived)
    q_crossed = gather_finish(all_q, q_arrived)
    lax.fori_loop(0, ROWS // 64, split_rows, 0)
    m_crossed.wait_recv()
    dense_m[...] = jnp.zeros((COARSE, COARSE + 256), F32)
    for block in range(SUBS):
        offset = 32 * (block - 1) + 128
        tile, shift = offset // 128, offset % 128
        rows = slice(block * MODES, (block + 1) * MODES)
        value = all_m[block % 2, block // 2]
        if shift:
            value = pltpu.roll(value, shift, 1)
        lane = lax.broadcasted_iota(jnp.int32, (MODES, 128), 1)
        dense_m[rows, tile * 128 : (tile + 1) * 128] = jnp.where(lane >= shift, value, 0.0)
        if shift:
            dense_m[rows, (tile + 1) * 128 : (tile + 2) * 128] = jnp.where(
                lane < shift, value, 0.0
            )
    square_m = dense_m[:, 128 : 128 + COARSE]
    inner = coarse[MODES : MODES + COARSE, :]
    mixed[:, 0:128] = near
    mixed[:, 128:256] = near - exact(inner, exact(square_m, near))
    for block in range(SUBS):
        to = ((block % 2) * 8 + block // 2) * 16
        table_even[to : to + 16, :] = mixed[block * MODES : block * MODES + 16, :]
        table_odd[to : to + 16, :] = mixed[block * MODES + 16 : (block + 1) * MODES, :]

    def coefficients(buffer):
        turned = buffer[...].reshape(SUBS * 16, 128).T
        return exact(turned[:COLS], table_even[...]) + exact(
            turned[COLS:], table_odd[...]
        )

    def project_pair(value, value_proj, factors, source):
        lift = exact(
            jnp.concatenate([factors[:, :128], factors[:, 128:]], axis=0),
            moments_map[...],
        )
        once = source[:, :PAIR] - lift[:COLS]
        value[:, :PAIR] = once
        value_proj[:, :PAIR] = once - lift[COLS:]
        value[:, PAIR:] = source[:, PAIR:]
        value_proj[:, PAIR:] = source[:, PAIR:]

    q_crossed.wait_recv()
    project_pair(dirs, proj, coefficients(all_q), first)

    def reduce_all(bufs, value):
        mates, along_x, along_y, along_z, halves = bufs
        rows = value.shape[0] // 2
        mates[core, 0] = value[:rows]
        mates[core, 1] = value[rows:]
        copy = swap(mates.at[core, 1 - core], mates.at[core, 1 - core], (c, mate))
        yield
        copy.wait_recv()
        along_x[x] = mates[0, core] + mates[1, core]
        arrived = share(along_x, x, x_peers)
        yield
        arrived.wait()
        along_y[y] = (along_x[0] + along_x[1]) + (along_x[2] + along_x[3])
        arrived = share(along_y, y, y_peers)
        yield
        arrived.wait()
        along_z[z] = (along_y[0] + along_y[1]) + (along_y[2] + along_y[3])
        arrived = share(along_z, z, z_peers)
        yield
        arrived.wait()
        total = along_z[0]
        for i in range(1, 8):
            total = total + along_z[i]
        halves[core] = total
        copy = swap(halves.at[core], halves.at[core], (c, mate))
        yield
        copy.wait_recv()
        yield jnp.concatenate([halves[0], halves[1]], axis=0)

    def dual(source, halos, outs, nears, sides_out, alls):
        high_x, low_x = split(source[...] * weights[0:1, :])
        both = single(jnp.concatenate([high_x, low_x], axis=0), scatter[...]).astype(BF16)
        turned = single(both, high[...])
        image_local = turned[:COLS] + turned[COLS:] + single(both[:COLS], low[...])
        high_f, low_f = split(image_local)
        back = single(jnp.concatenate([high_f, low_f], axis=0), gather[...])
        back = (back[:COLS] + back[COLS:]) * weights[0:1, :]
        halo_copies = []
        for side in range(4):
            sides_out[side] = back[:, part(side)]
        shares = exact(moments_map[...], back[:, :PAIR], NT)
        outs[0] = fold(shares[0:MODES])
        outs[1] = fold(shares[2 * MODES : 3 * MODES])
        near_copies = [
            swap(outs.at[0], nears.at[1], (c, down)),
            swap(outs.at[1], nears.at[0], (c, up)),
        ]
        for side in range(4):
            halo_copies.append(
                swap(sides_out.at[side], halos.at[FACING[side]], side_peers[side])
            )
        energy = exact(
            both[:COLS].astype(F32) + both[COLS:].astype(F32), image_local, NT
        )
        return energy, fold(shares[MODES : 2 * MODES]), near_copies, halo_copies

    def finish_image(halos, sides_out, factors, halo_copies):
        for copy in halo_copies:
            copy.wait_recv()
        for side in range(4):
            local[:, part(side)] = sides_out[side] + halos[side]
        project_pair(image, image_proj, factors, local)

    def eliminate(value):
        square[...] = value
        lane = lax.broadcasted_iota(jnp.int32, (COLS, 2 * COLS), 1)
        row = lax.broadcasted_iota(jnp.int32, (COLS, 2 * COLS), 0)

        def step(k, carry):
            table = square[...]
            line = square[pl.ds(k, 1), :]
            column = jnp.sum(jnp.where(lane == k, table, 0.0), axis=1, keepdims=True)
            pivot = jnp.sum(jnp.where(lane[0:1] == k, line, 0.0), axis=1, keepdims=True)
            line = line / pivot
            square[...] = jnp.where(row == k, line, table - column * line)
            return carry

        lax.fori_loop(0, COLS, step, 0)
        return square[:, COLS:]

    start_gram = 0.5 * exact(dirs[...], dirs[...], NT)
    energy, own_part, near_copies, halo_copies = dual(
        proj, halo_one, out_one, near_one, far_one, all_one
    )
    reduction = reduce_all(sum_a, jnp.concatenate([energy, start_gram], axis=1))
    next(reduction)
    for copy in near_copies:
        copy.wait_recv()
    arrived = gather_start(all_one, own_part + near_one[0] + near_one[1])
    next(reduction)
    crossed = gather_finish(all_one, arrived)
    next(reduction)
    crossed.wait_recv()
    finish_image(halo_one, far_one, coefficients(all_one), halo_copies)
    norm = 0.5 * exact(image[...], image[...], NT)
    next(reduction)
    second = reduce_all(sum_b, fold(norm))
    next(second)
    next(reduction)
    next(second)
    both_grams = next(reduction)
    curvature, descent = both_grams[:, :COLS], both_grams[:, COLS:]
    row = lax.broadcasted_iota(jnp.int32, (COLS, COLS), 0)
    lane = lax.broadcasted_iota(jnp.int32, (COLS, COLS), 1)
    identity = jnp.where(row == lane, 1.0, 0.0)
    inverse = eliminate(jnp.concatenate([curvature, identity], axis=1))
    step_t = exact(descent, inverse)
    next(second)
    next(second)
    next(second)
    norm = unfold(next(second))
    blend = exact(exact(step_t, norm), inverse)

    for side in range(4):
        at = part(side)
        start, moved = dirs[:, at], exact(step_t, image[:, at])
        resid[:, at] = start - moved
        first[:, at] = exact(step_t, start)
        dirs[:, at] = exact(blend, start) - moved
        proj[:, at] = exact(blend, proj[:, at]) - exact(step_t, image_proj[:, at])

    start_gram = 0.5 * exact(dirs[...], resid[...], NT)
    energy, own_part, near_copies, halo_copies = dual(
        proj, halo_two, out_two, near_two, far_two, all_two
    )
    reduction = reduce_all(sum_c, jnp.concatenate([energy, start_gram], axis=1))
    next(reduction)
    for copy in near_copies:
        copy.wait_recv()
    arrived = gather_start(all_two, own_part + near_two[0] + near_two[1])
    next(reduction)
    crossed = gather_finish(all_two, arrived)
    next(reduction)
    crossed.wait_recv()
    finish_image(halo_two, far_two, coefficients(all_two), halo_copies)
    next(reduction)
    next(reduction)
    step_t = eliminate(next(reduction)).T

    for side in range(4):
        at = part(side)
        rows = slice(side * FACE, (side + 1) * FACE)
        result = resid[:, at] - exact(step_t, image[:, at])
        out_res[rows, :] = result.T[:FACE]
        result = first[:, at] + exact(step_t, dirs[:, at])
        out_sol[rows, :] = result.T[:FACE]
    stores = [
        pltpu.make_async_copy(out_sol, sol_hbm.at[0, 0], local_sem.at[4]),
        pltpu.make_async_copy(out_res, res_hbm.at[0, 0], local_sem.at[5]),
    ]
    for store in stores:
        store.start()
    for wait in pending:
        wait()
    for store in stores:
        store.wait()


def shards(*arguments):
    def vmem(*shape, dtype=F32):
        return pltpu.VMEM(shape, dtype)

    def sums(rows):
        return (
            vmem(2, 2, rows, 128), vmem(4, rows, 128), vmem(4, rows, 128),
            vmem(8, rows, 128), vmem(2, rows, 128),
        )

    vector = vmem(COLS, WIDE)
    moments = vmem(2, 8, 16, 128)
    anywhere = pl.BlockSpec(memory_space=pl.ANY)
    out = jax.ShapeDtypeStruct((1, 1, ROWS, COLS), F32)
    return tuple(
        pl.pallas_call(
            kernel,
            out_shape=(out, out),
            in_specs=[
                anywhere, anywhere, pl.BlockSpec(memory_space=pltpu.SMEM),
                pl.BlockSpec(memory_space=pltpu.VMEM), anywhere, anywhere,
            ],
            out_specs=(anywhere, anywhere),
            scratch_shapes=[
                vmem(ROWS, ROWS), vmem(ROWS, ROWS, dtype=BF16), vmem(ROWS, ROWS, dtype=BF16),
                vmem(WIDE, ROWS, dtype=BF16), vmem(ROWS, WIDE, dtype=BF16),
                vmem(ROWS, COLS), vmem(4, FACE, COLS), vmem(MODES, 2 * FACE),
                vmem(2, MODES, 2 * FACE), vmem(COARSE + 3 * MODES, COARSE),
                vmem(4 * MODES, PAIR),
                vmem(8, WIDE), vector, vector, vector, vector, vector, vector, vector,
                vmem(4, COLS, SIDE), vmem(4, COLS, SIDE), vmem(2, 16, 128), vmem(2, 16, 128),
                vmem(2, 16, 128), vmem(2, 16, 128), vmem(4, COLS, SIDE), vmem(4, COLS, SIDE),
                moments, vmem(2, 8, MODES, 128), moments, moments,
                vmem(COARSE, 256), vmem(256, 256), vmem(256, 256), vmem(COARSE, COARSE + 256),
                sums(32), sums(16), sums(32), vmem(COLS, 128), vmem(ROWS, COLS), vmem(ROWS, COLS),
                pltpu.SemaphoreType.DMA((6,)), pltpu.SemaphoreType.DMA((64,)),
                pltpu.SemaphoreType.DMA((64,)),
            ],
            compiler_params=pltpu.CompilerParams(
                collective_id=0, has_side_effects=True, vmem_limit_bytes=60 * 1024 * 1024
            ),
        )(*arguments)
    )


def solution(mesh):
    return jax.shard_map(
        shards,
        mesh=mesh,
        in_specs=(
            P("cluster", "sub", None, None),
            P("cluster", "sub", None, None),
            P("cluster", "sub", None),
            P("cluster", "sub", None),
            P("cluster", "sub", None, None),
            P("cluster", None, None),
        ),
        out_specs=(P("cluster", "sub", None, None), P("cluster", "sub", None, None)),
        check_vma=False,
    )
```

```python
import jax
import jax.numpy as jnp
from jax import lax
from jax.sharding import PartitionSpec as P
from jax.experimental import pallas as pl
from jax.experimental.pallas import tpu as pltpu


ROWS = 1408
FACE = 352
SIDE = 384
WIDE = 4 * SIDE
PAIR = 2 * SIDE
COLS = 64
MODES = 32
SUBS = 16
COARSE = 512
SIGNS = (-1.0, 1.0, -1.0, 1.0)
WINDOWS = ((0, 384), (256, 512), (640, 512), (1024, 384))
FACING = (1, 0, 3, 2)

F32 = jnp.float32
BF16 = jnp.bfloat16
NN = (((1,), (0,)), ((), ()))
NT = (((1,), (1,)), ((), ()))


def exact(left, right, dims=NN):
    return lax.dot_general(
        left, right, dims, precision=lax.Precision.HIGHEST, preferred_element_type=F32
    )


def single(left, right):
    return lax.dot_general(left, right, NN, preferred_element_type=F32)


def split(value):
    high = value.astype(BF16)
    return high, (value - high.astype(F32)).astype(BF16)


def fold(value):
    half = value.shape[0] // 2
    return jnp.concatenate([value[:half], value[half:]], axis=1)


def unfold(value):
    half = value.shape[1] // 2
    return jnp.concatenate([value[:, :half], value[:, half:]], axis=0)


def part(side):
    return slice(side * SIDE, (side + 1) * SIDE)


def eliminate(left, right):
    joined = jnp.concatenate([left, right], axis=1)
    table = [joined[8 * r : 8 * r + 8] for r in range(8)]
    row = lax.broadcasted_iota(jnp.int32, (8, 2 * COLS), 0)
    for block in range(8):
        columns = [
            [
                jnp.broadcast_to(rows[:, 8 * block + j : 8 * block + j + 1], (8, 2 * COLS))
                for j in range(8)
            ]
            for rows in table
        ]
        panel, own = table[block], columns[block]
        for j in range(8):
            scale = 1.0 / own[j][j : j + 1]
            line = panel[j : j + 1] * scale
            panel = jnp.where(row == j, line, panel - own[j] * line)
            for k in range(j + 1, 8):
                entry = own[k][j : j + 1] * scale
                own[k] = jnp.where(row == j, entry, own[k] - own[j] * entry)
        for r in range(8):
            if r == block:
                table[r] = panel
            else:
                for j in range(8):
                    table[r] = table[r] - columns[r][j] * panel[j : j + 1]
    return jnp.concatenate(table, axis=0)[:, COLS:]


def kernel(
    ops_hbm, contrib_hbm, sizes, map_ref, basis_hbm, coarse_hbm,
    sol_hbm, res_hbm,
    full, high, low, scatter, gather, moments_slots,
    own_rhs, halo_rhs, own_basis, near_basis, coarse, moments_map,
    weights, first, basis, proj, image_proj, local,
    halo_one, halo_two, near_one, near_two, out_one, out_two, far_one, far_two,
    all_q, all_m, all_one, all_two, mixed, table_even, table_odd, dense_m,
    sum_a, sum_b, sum_c, out_sol, out_res,
    local_sem, send_sem, recv_sem,
):
    c, s = lax.axis_index("cluster"), lax.axis_index("sub")
    x, y = lax.div(c, 4), lax.rem(c, 4)
    z, core = lax.div(s, 2), lax.rem(s, 2)
    down, up = lax.rem(s + SUBS - 1, SUBS), lax.rem(s + 1, SUBS)
    west, east = lax.rem(c + 15, 16), lax.rem(c + 1, 16)
    mate = z * 2 + 1 - core
    x_peers = [(lax.rem(x + i, 4) * 4 + y, s) for i in range(1, 4)]
    y_peers = [(x * 4 + lax.rem(y + i, 4), s) for i in range(1, 4)]
    z_peers = [(c, lax.rem(z + i, 8) * 2 + core) for i in range(1, 8)]
    side_peers = ((c, down), (c, up), (west, s), (east, s))
    used = [0]

    def fresh():
        used[0] += 1
        return used[0] - 1

    loads = [
        pltpu.make_async_copy(contrib_hbm.at[0, 0], own_rhs, local_sem.at[0]),
        pltpu.make_async_copy(basis_hbm.at[0, 0], own_basis, local_sem.at[1]),
        pltpu.make_async_copy(
            coarse_hbm.at[0], coarse.at[pl.ds(MODES, COARSE)], local_sem.at[2]
        ),
        pltpu.make_async_copy(ops_hbm.at[0, 0], full, local_sem.at[3]),
    ]
    for load in loads:
        load.start()

    barrier = pltpu.get_barrier_semaphore()
    greeted = [(c, mate)] + z_peers + x_peers + y_peers
    greeted += [(c, down), (c, up), (west, s), (east, s)]
    for peer in greeted:
        pl.semaphore_signal(
            barrier, inc=1, device_id=peer, device_id_type=pl.DeviceIdType.MESH
        )
    pl.semaphore_wait(barrier, len(greeted))

    def send(source, target, peer, slot):
        copy = pltpu.make_async_remote_copy(
            src_ref=source, dst_ref=target,
            send_sem=send_sem.at[slot], recv_sem=recv_sem.at[slot],
            device_id=peer, device_id_type=pl.DeviceIdType.MESH,
        )
        copy.start()
        return copy

    pending = []

    def share(buffer, me, peers):
        slot = fresh()
        for peer in peers:
            send(buffer.at[me], buffer.at[me], peer, slot)
        whole = buffer.at[pl.ds(0, len(peers))]
        pending.append(lambda: pltpu.make_async_copy(whole, whole, send_sem.at[slot]).wait())
        return pltpu.make_async_copy(whole, whole, recv_sem.at[slot])

    def swap(source, target, peer):
        copy = send(source, target, peer, fresh())
        pending.append(copy.wait_send)
        return copy

    rhs_copies = []
    for side in range(4):
        start, length = WINDOWS[side]
        rhs_copies.append(
            swap(
                contrib_hbm.at[0, 0, :, pl.ds(start, length)],
                halo_rhs.at[FACING[side], :, pl.ds(0, length)],
                side_peers[side],
            )
        )
    basis_copies = [
        swap(basis_hbm.at[0, 0], near_basis.at[1], (c, down)),
        swap(basis_hbm.at[0, 0], near_basis.at[0], (c, up)),
    ]

    slots = map_ref[0]
    slots = slots + (SIDE - FACE) * (
        (slots >= FACE).astype(jnp.int32)
        + (slots >= 2 * FACE).astype(jnp.int32)
        + (slots >= 3 * FACE).astype(jnp.int32)
    )

    def fill_scatter(step, carry):
        rows = pl.ds(pl.multiple_of(step * 128, 128), 128)
        index = lax.broadcasted_iota(jnp.int32, (128, ROWS), 0) + step * 128
        scatter[rows, :] = jnp.where(index == slots, 1.0, 0.0).astype(BF16)
        return carry

    lax.fori_loop(0, WIDE // 128, fill_scatter, 0)
    lanes = lax.broadcasted_iota(jnp.int32, (8, SIDE), 1)
    for side in range(4):
        weights[:, part(side)] = jnp.where(lanes < sizes[0, 0, side], SIGNS[side], 0.0)

    loads[1].wait()
    zero_lanes = jnp.zeros((MODES, SIDE - FACE), F32)

    def half_basis(value, side):
        return jnp.concatenate(
            [value[:, side * FACE : (side + 1) * FACE], zero_lanes], axis=1
        )

    weight_low, weight_high = weights[0:1, part(0)], weights[0:1, part(1)]
    empty = jnp.zeros((MODES, SIDE), F32)
    mine = own_basis[...]
    moments_map[MODES : 2 * MODES, part(0)] = half_basis(mine, 0) * weight_low
    moments_map[MODES : 2 * MODES, part(1)] = half_basis(mine, 1) * weight_high
    for copy in basis_copies:
        copy.wait_recv()
    moments_map[0:MODES, part(0)] = -half_basis(near_basis[0], 1) * weight_low
    moments_map[0:MODES, part(1)] = empty
    moments_map[2 * MODES : 3 * MODES, part(0)] = empty
    moments_map[2 * MODES : 3 * MODES, part(1)] = (
        -half_basis(near_basis[1], 0) * weight_high
    )
    moments_map[3 * MODES : 4 * MODES, :] = jnp.zeros((MODES, PAIR), F32)

    def gather_start(buffer, value):
        buffer[core, z] = value
        return share(buffer.at[core], z, z_peers)

    def gather_finish(buffer, arrived):
        arrived.wait()
        return swap(buffer.at[core], buffer.at[core], (c, mate))

    loads[0].wait()
    for copy in rhs_copies:
        copy.wait_recv()
    index = lax.broadcasted_iota(jnp.int32, (COLS, FACE), 1)
    zero_columns = jnp.zeros((COLS, SIDE - FACE), F32)
    for side in range(4):
        shift = FACING[side] * FACE - WINDOWS[FACING[side]][0]
        own = own_rhs[:, side * FACE : (side + 1) * FACE]
        other = halo_rhs[side][:, shift : shift + FACE]
        joined = jnp.where(index < sizes[0, 0, side], SIGNS[side] * (own - other), 0.0)
        first[:, part(side)] = jnp.concatenate([joined, zero_columns], axis=1)
    q_moments = exact(moments_map[MODES : 2 * MODES, :], first[:, :PAIR], NT)
    q_arrived = gather_start(all_q, fold(q_moments))
    m_own = exact(moments_map[MODES : 2 * MODES, :], moments_map[...], NT)
    m_own = jnp.concatenate(
        [0.5 * m_own[:, MODES : 2 * MODES], m_own[:, 2 * MODES : 3 * MODES]], axis=1
    )
    m_arrived = gather_start(all_m, fold(m_own))

    columns = lax.broadcasted_iota(jnp.int32, (128, 128), 1).astype(F32)
    for step in range(ROWS // 128):
        piece = slots[:, step * 128 : (step + 1) * 128].astype(F32)
        tall = jnp.broadcast_to(piece, (128, 128)).T
        for tile in range(WIDE // 128):
            gather[step * 128 : (step + 1) * 128, tile * 128 : (tile + 1) * 128] = (
                jnp.where(tall == columns + float(tile * 128), 1.0, 0.0).astype(BF16)
            )

    def split_rows(step, carry):
        rows = pl.ds(pl.multiple_of(step * 64, 64), 64)
        high[rows, :], low[rows, :] = split(full[rows, :])
        return carry

    map_high, map_low = split(moments_map[...] * weights[0:1, :PAIR])
    spread = single(jnp.concatenate([map_high, map_low], axis=0), scatter[:PAIR, :])
    map_high, map_low = split(spread[: 4 * MODES] + spread[4 * MODES :])
    moments_slots[: 4 * MODES] = map_high
    moments_slots[4 * MODES :] = map_low

    loads[2].wait()
    coarse[0:MODES, :] = jnp.zeros((MODES, COARSE), F32)
    coarse[MODES + COARSE :, :] = jnp.zeros((2 * MODES, COARSE), F32)
    near_rows = coarse[pl.ds(pl.multiple_of(s * MODES, MODES), 4 * MODES), :]
    near = near_rows.T
    dense_m[...] = jnp.zeros((COARSE, COARSE + 128), F32)

    q_crossed = gather_finish(all_q, q_arrived)
    m_crossed = gather_finish(all_m, m_arrived)
    loads[3].wait()
    lax.fori_loop(0, ROWS // 64, split_rows, 0)
    m_crossed.wait_recv()
    lane = lax.broadcasted_iota(jnp.int32, (MODES, 128), 1)
    blank = jnp.zeros((MODES, 64), F32)
    for block in range(SUBS):
        tile, shift = block // 4, 32 * (block % 4)
        rows = slice(block * MODES, (block + 1) * MODES)
        value = jnp.concatenate([unfold(all_m[block % 2, block // 2]), blank], axis=1)
        if shift:
            value = pltpu.roll(value, shift, 1)
        if shift == 96:
            dense_m[rows, (tile + 1) * 128 : (tile + 2) * 128] = jnp.where(
                lane < shift, value, 0.0
            )
            value = jnp.where(lane >= shift, value, 0.0)
        dense_m[rows, tile * 128 : (tile + 1) * 128] = value
    square_m = dense_m[:, :COARSE]
    square_m = square_m + square_m.T
    inner = coarse[MODES : MODES + COARSE, :]
    mixed[:, 0:128] = near
    mixed[:, 128:256] = near - exact(inner, exact(square_m, near))
    for block in range(SUBS):
        to = ((block % 2) * 8 + block // 2) * 16
        table_even[to : to + 16, :] = mixed[block * MODES : block * MODES + 16, :]
        table_odd[to : to + 16, :] = mixed[block * MODES + 16 : (block + 1) * MODES, :]

    def coefficients(buffer):
        turned = buffer[...].reshape(SUBS * 16, 128).T
        return exact(turned[:COLS], table_even[...]) + exact(
            turned[COLS:], table_odd[...]
        )

    def place(which):
        return slice(which * COLS, (which + 1) * COLS)

    def project_pair(which, value_proj, factors, source):
        lift = exact(
            jnp.concatenate([factors[:, :128], factors[:, 128:]], axis=0),
            moments_map[...],
        )
        once = source[:, :PAIR] - lift[:COLS]
        basis[place(which), :PAIR] = once
        value_proj[:, :PAIR] = once - lift[COLS:]
        basis[place(which), PAIR:] = source[:, PAIR:]
        value_proj[:, PAIR:] = source[:, PAIR:]

    q_crossed.wait_recv()
    project_pair(0, proj, coefficients(all_q), first)

    def reduce_all(bufs, value):
        mates, along_x, along_y, along_z, halves = bufs
        rows = value.shape[0] // 2
        mates[core, 0] = value[:rows]
        mates[core, 1] = value[rows:]
        copy = swap(mates.at[core, 1 - core], mates.at[core, 1 - core], (c, mate))
        yield
        copy.wait_recv()
        along_x[x] = mates[0, core] + mates[1, core]
        arrived = share(along_x, x, x_peers)
        yield
        arrived.wait()
        along_y[y] = (along_x[0] + along_x[1]) + (along_x[2] + along_x[3])
        arrived = share(along_y, y, y_peers)
        yield
        arrived.wait()
        along_z[z] = (along_y[0] + along_y[1]) + (along_y[2] + along_y[3])
        arrived = share(along_z, z, z_peers)
        yield
        arrived.wait()
        total = along_z[0]
        for i in range(1, 8):
            total = total + along_z[i]
        halves[core] = total
        copy = swap(halves.at[core], halves.at[core], (c, mate))
        yield
        copy.wait_recv()
        yield jnp.concatenate([halves[0], halves[1]], axis=0)

    def three_parts(value):
        high_v = value.astype(BF16)
        rest = value - high_v.astype(F32)
        return jnp.concatenate((high_v,) + split(rest), axis=0)

    def spread_slots(source):
        return single(three_parts(source[...] * weights[0:1, :]), scatter[...]).astype(BF16)

    def product(both):
        turned, small = single(both, high[...]), single(both[: 2 * COLS], low[...])
        return turned[:COLS] + (
            (turned[COLS : 2 * COLS] + small[:COLS])
            + (turned[2 * COLS :] + small[COLS:])
        )

    def energy(both, value):
        whole = both.astype(F32)
        whole = whole[:COLS] + (whole[COLS : 2 * COLS] + whole[2 * COLS :])
        return exact(whole, value, NT)

    def send_moments(parts, outs, nears):
        both = lax.dot_general(
            moments_slots[...], parts[: 2 * COLS], NT, preferred_element_type=F32
        )
        half = 4 * MODES
        shares = both[:half, :COLS] + both[half:, :COLS] + both[:half, COLS:]
        outs[0] = fold(shares[0:MODES])
        outs[1] = fold(shares[2 * MODES : 3 * MODES])
        copies = [
            swap(outs.at[0], nears.at[1], (c, down)),
            swap(outs.at[1], nears.at[0], (c, up)),
        ]
        return fold(shares[MODES : 2 * MODES]), copies

    def send_sides(parts, halos, sides_out):
        back = single(parts, gather[...])
        back = back[:COLS] + (back[COLS : 2 * COLS] + back[2 * COLS :])
        back = back * weights[0:1, :]
        copies = []
        for side in (2, 3, 0, 1):
            sides_out[side] = back[:, part(side)]
            copies.append(
                swap(sides_out.at[side], halos.at[FACING[side]], side_peers[side])
            )
        return copies

    def both_parts(value):
        return jnp.concatenate(split(value), axis=0)

    def join_sides(halos, sides_out, copies):
        for copy in copies:
            copy.wait_recv()
        for side in range(4):
            local[:, part(side)] = sides_out[side] + halos[side]

    spread = spread_slots(proj)
    value = product(spread)
    parts = three_parts(value)
    own_part, near_copies = send_moments(parts, out_one, near_one)
    halo_copies = send_sides(parts, halo_one, far_one)
    curvature = energy(spread, value)
    start = basis[place(0), :]
    descent = 0.5 * exact(start, start, NT)
    reduction = reduce_all(sum_a, jnp.concatenate([curvature, descent], axis=1))
    next(reduction)
    for copy in near_copies:
        copy.wait_recv()
    arrived = gather_start(all_one, own_part + near_one[0] + near_one[1])
    next(reduction)
    join_sides(halo_one, far_one, halo_copies)
    next(reduction)
    crossed = gather_finish(all_one, arrived)
    next(reduction)
    crossed.wait_recv()
    project_pair(1, image_proj, coefficients(all_one), local)
    image = basis[place(1), :]
    second = reduce_all(sum_b, fold(0.5 * exact(image, image, NT)))
    next(second)

    spread = spread_slots(image_proj)
    next(second)
    value = product(spread)
    third = reduce_all(sum_c, fold(energy(spread, value)))
    next(third)
    next(second)
    next(reduction)
    parts = three_parts(value)
    own_part, near_copies = send_moments(parts, out_two, near_two)
    next(third)
    halo_copies = send_sides(parts, halo_two, far_two)
    both_grams = next(reduction)
    curvature, descent = both_grams[:, :COLS], both_grams[:, COLS:]
    next(second)
    row = lax.broadcasted_iota(jnp.int32, (COLS, COLS), 0)
    lane = lax.broadcasted_iota(jnp.int32, (COLS, COLS), 1)
    inverse = eliminate(curvature, jnp.where(row == lane, 1.0, 0.0))
    next(third)
    for copy in near_copies:
        copy.wait_recv()
    arrived = gather_start(all_two, own_part + near_two[0] + near_two[1])
    alpha, alpha_t = exact(inverse, descent), exact(descent, inverse)
    next(second)
    next(third)
    norm = unfold(next(second))
    moved = exact(norm, alpha)
    blend = exact(inverse, moved)
    known = exact(alpha_t, exact(norm, blend))
    descent_two = exact(alpha_t, moved) - descent
    crossed = gather_finish(all_two, arrived)
    join_sides(halo_two, far_two, halo_copies)
    crossed.wait_recv()
    factors = coefficients(all_two)
    lift = exact(factors[:, :128], moments_map[...])
    basis[place(2), :PAIR] = local[:, :PAIR] - lift
    basis[place(2), PAIR:] = local[:, PAIR:]
    next(third)
    cubic = unfold(next(third))

    curvature_two = exact(alpha_t, exact(cubic, alpha)) - known
    alpha_two = eliminate(curvature_two, descent_two)
    outer = (alpha + exact(blend, alpha_two)).T
    cross = exact(alpha, alpha_two).T
    none = jnp.zeros((COLS, COLS), F32)
    mix = jnp.concatenate(
        [
            jnp.concatenate([outer, -cross, none], axis=1),
            jnp.concatenate([none, -outer, cross], axis=1),
        ],
        axis=0,
    )
    for side in range(4):
        result = exact(mix, basis[:, part(side)])
        at = slice(side * FACE, (side + 1) * FACE)
        out_sol[:, at] = result[:COLS, :FACE]
        out_res[:, at] = (basis[place(0), part(side)] + result[COLS:])[:, :FACE]
    stores = [
        pltpu.make_async_copy(out_sol, sol_hbm.at[0, 0], local_sem.at[4]),
        pltpu.make_async_copy(out_res, res_hbm.at[0, 0], local_sem.at[5]),
    ]
    for store in stores:
        store.start()
    for wait in pending:
        wait()
    for store in stores:
        store.wait()


def shards(dual_ops, contributions, block_sizes, mult_map, coarse_basis, coarse_inverse):
    def vmem(*shape, dtype=F32):
        return pltpu.VMEM(shape, dtype)

    def sums(rows):
        return (
            vmem(2, 2, rows, 128), vmem(4, rows, 128), vmem(4, rows, 128),
            vmem(8, rows, 128), vmem(2, rows, 128),
        )

    vector = vmem(COLS, WIDE)
    moments = vmem(2, 8, 16, 128)
    sides, pair = vmem(4, COLS, SIDE), vmem(2, 16, 128)
    anywhere = pl.BlockSpec(memory_space=pl.ANY)
    out = jax.ShapeDtypeStruct((1, 1, COLS, ROWS), F32)
    results = pl.pallas_call(
        kernel,
        out_shape=(out, out),
        in_specs=[
            anywhere, anywhere, pl.BlockSpec(memory_space=pltpu.SMEM),
            pl.BlockSpec(memory_space=pltpu.VMEM), anywhere, anywhere,
        ],
        out_specs=(anywhere, anywhere),
        scratch_shapes=[
            vmem(ROWS, ROWS), vmem(ROWS, ROWS, dtype=BF16), vmem(ROWS, ROWS, dtype=BF16),
            vmem(WIDE, ROWS, dtype=BF16), vmem(ROWS, WIDE, dtype=BF16),
            vmem(8 * MODES, ROWS, dtype=BF16),
            vmem(COLS, ROWS), vmem(4, COLS, 512), vmem(MODES, 2 * FACE),
            vmem(2, MODES, 2 * FACE), vmem(COARSE + 3 * MODES, COARSE),
            vmem(4 * MODES, PAIR),
            vmem(8, WIDE), vector, vmem(3 * COLS, WIDE), vector, vector, vector,
            sides, sides, pair, pair, pair, pair, sides, sides,
            moments, moments, moments, moments,
            vmem(COARSE, 256), vmem(256, 256), vmem(256, 256), vmem(COARSE, COARSE + 128),
            sums(32), sums(16), sums(16), vmem(COLS, ROWS), vmem(COLS, ROWS),
            pltpu.SemaphoreType.DMA((6,)), pltpu.SemaphoreType.DMA((64,)),
            pltpu.SemaphoreType.DMA((64,)),
        ],
        compiler_params=pltpu.CompilerParams(
            collective_id=0, has_side_effects=True, vmem_limit_bytes=60 * 1024 * 1024
        ),
    )(
        dual_ops, jnp.swapaxes(contributions, 2, 3), block_sizes, mult_map,
        coarse_basis, coarse_inverse,
    )
    return tuple(jnp.swapaxes(result, 2, 3) for result in results)


def solution(mesh):
    return jax.shard_map(
        shards,
        mesh=mesh,
        in_specs=(
            P("cluster", "sub", None, None),
            P("cluster", "sub", None, None),
            P("cluster", "sub", None),
            P("cluster", "sub", None),
            P("cluster", "sub", None, None),
            P("cluster", None, None),
        ),
        out_specs=(P("cluster", "sub", None, None), P("cluster", "sub", None, None)),
        check_vma=False,
    )
```

```python
import jax
import jax.numpy as jnp
from jax import lax
from jax.sharding import PartitionSpec as P
from jax.experimental import pallas as pl
from jax.experimental.pallas import tpu as pltpu


ROWS = 1408
FACE = 352
SIDE = 384
WIDE = 4 * SIDE
PAIR = 2 * SIDE
COLS = 64
MODES = 32
SUBS = 16
COARSE = 512
SIGNS = (-1.0, 1.0, -1.0, 1.0)
FACING = (1, 0, 3, 2)

F32 = jnp.float32
BF16 = jnp.bfloat16
NN = (((1,), (0,)), ((), ()))
NT = (((1,), (1,)), ((), ()))


def exact(left, right, dims=NN):
    return lax.dot_general(
        left, right, dims, precision=lax.Precision.HIGHEST, preferred_element_type=F32
    )


def single(left, right):
    return lax.dot_general(left, right, NN, preferred_element_type=F32)


def split(value):
    high = value.astype(BF16)
    return high, (value - high.astype(F32)).astype(BF16)


def fold(value):
    half = value.shape[0] // 2
    return jnp.concatenate([value[:half], value[half:]], axis=1)


def unfold(value):
    half = value.shape[1] // 2
    return jnp.concatenate([value[:, :half], value[:, half:]], axis=0)


def part(side):
    return slice(side * SIDE, (side + 1) * SIDE)


def eliminate(left, right):
    joined = jnp.concatenate([left, right], axis=1)
    table = [joined[8 * r : 8 * r + 8] for r in range(8)]
    row = lax.broadcasted_iota(jnp.int32, (8, 2 * COLS), 0)
    for block in range(8):
        columns = [
            [
                jnp.broadcast_to(rows[:, 8 * block + j : 8 * block + j + 1], (8, 2 * COLS))
                for j in range(8)
            ]
            for rows in table
        ]
        panel, own = table[block], columns[block]
        for j in range(8):
            scale = 1.0 / own[j][j : j + 1]
            line = panel[j : j + 1] * scale
            panel = jnp.where(row == j, line, panel - own[j] * line)
            for k in range(j + 1, 8):
                entry = own[k][j : j + 1] * scale
                own[k] = jnp.where(row == j, entry, own[k] - own[j] * entry)
        for r in range(8):
            if r == block:
                table[r] = panel
            else:
                for j in range(8):
                    table[r] = table[r] - columns[r][j] * panel[j : j + 1]
    return jnp.concatenate(table, axis=0)[:, COLS:]


def kernel(
    ops_hbm, contrib_hbm, sizes, map_ref, basis_hbm, coarse_hbm,
    sol_hbm, res_hbm,
    full, high, low, scatter, gather, moments_slots,
    own_rhs, halo_q, far_q, own_basis, half_basis, near_basis, coarse, moments_map,
    weights, first, basis, proj, image_proj, local,
    halo_one, halo_two, near_one, near_two, out_one, out_two, far_one, far_two,
    all_q, all_m, all_one, all_two, mixed, table_even, table_odd, dense_m,
    sum_a, sum_b, sum_c, out_sol, out_res,
    local_sem, send_sem, recv_sem,
):
    c, s = lax.axis_index("cluster"), lax.axis_index("sub")
    x, y = lax.div(c, 4), lax.rem(c, 4)
    z, core = lax.div(s, 2), lax.rem(s, 2)
    down, up = lax.rem(s + SUBS - 1, SUBS), lax.rem(s + 1, SUBS)
    west, east = lax.rem(c + 15, 16), lax.rem(c + 1, 16)
    mate = z * 2 + 1 - core
    x_peers = [(lax.rem(x + i, 4) * 4 + y, s) for i in (2, 1, 3)]
    x_others = [(lax.rem(x + i, 4) * 4 + y, mate) for i in (2, 1, 3, 0)]
    y_peers = [(x * 4 + lax.rem(y + i, 4), s) for i in (2, 1, 3)]
    z_peers = [(c, lax.rem(z + i, 8) * 2 + core) for i in (4, 3, 5, 2, 6, 1, 7)]
    side_peers = ((c, down), (c, up), (west, s), (east, s))
    used = [0]

    def fresh():
        used[0] += 1
        return used[0] - 1

    loads = [
        pltpu.make_async_copy(contrib_hbm.at[0, 0], own_rhs, local_sem.at[0]),
        pltpu.make_async_copy(basis_hbm.at[0, 0], own_basis, local_sem.at[1]),
        pltpu.make_async_copy(
            coarse_hbm.at[0], coarse.at[pl.ds(MODES, COARSE)], local_sem.at[2]
        ),
        pltpu.make_async_copy(ops_hbm.at[0, 0], full, local_sem.at[3]),
    ]
    for load in loads:
        load.start()

    barrier = pltpu.get_barrier_semaphore()
    greeted = z_peers + x_peers + x_others + y_peers
    greeted += [(c, down), (c, up), (west, s), (east, s)]
    for peer in greeted:
        pl.semaphore_signal(
            barrier, inc=1, device_id=peer, device_id_type=pl.DeviceIdType.MESH
        )

    lanes = lax.broadcasted_iota(jnp.int32, (8, SIDE), 1)
    for side in range(4):
        weights[:, part(side)] = jnp.where(lanes < sizes[0, 0, side], SIGNS[side], 0.0)
    loads[0].wait()
    zero_columns = jnp.zeros((COLS, SIDE - FACE), F32)
    for side in range(4):
        own = own_rhs[:, side * FACE : (side + 1) * FACE]
        far_q[side] = (
            jnp.concatenate([own, zero_columns], axis=1) * weights[0:1, part(side)]
        )
    loads[1].wait()
    zero_lanes = jnp.zeros((MODES, SIDE - FACE), F32)
    for side in range(2):
        own = own_basis[:, side * FACE : (side + 1) * FACE]
        half_basis[side] = jnp.concatenate([own, zero_lanes], axis=1)
    pl.semaphore_wait(barrier, len(greeted))

    def send(source, target, peer, slot):
        copy = pltpu.make_async_remote_copy(
            src_ref=source, dst_ref=target,
            send_sem=send_sem.at[slot], recv_sem=recv_sem.at[slot],
            device_id=peer, device_id_type=pl.DeviceIdType.MESH,
        )
        copy.start()
        return copy

    pending = []

    def share(buffer, me, peers):
        slot = fresh()
        for peer in peers:
            send(buffer.at[me], buffer.at[me], peer, slot)
        whole = buffer.at[pl.ds(0, len(peers))]
        pending.append(lambda: pltpu.make_async_copy(whole, whole, send_sem.at[slot]).wait())
        return pltpu.make_async_copy(whole, whole, recv_sem.at[slot])

    def swap(source, target, peer):
        copy = send(source, target, peer, fresh())
        pending.append(copy.wait_send)
        return copy

    basis_copies = [
        swap(half_basis.at[0], near_basis.at[1], (c, down)),
        swap(half_basis.at[1], near_basis.at[0], (c, up)),
    ]
    rhs_copies = [
        swap(far_q.at[side], halo_q.at[FACING[side]], side_peers[side])
        for side in (2, 3, 0, 1)
    ]

    slots = map_ref[0]
    slots = slots + (SIDE - FACE) * (
        (slots >= FACE).astype(jnp.int32)
        + (slots >= 2 * FACE).astype(jnp.int32)
        + (slots >= 3 * FACE).astype(jnp.int32)
    )

    def fill_scatter(step, carry):
        rows = pl.ds(pl.multiple_of(step * 128, 128), 128)
        index = lax.broadcasted_iota(jnp.int32, (128, ROWS), 0) + step * 128
        scatter[rows, :] = jnp.where(index == slots, 1.0, 0.0).astype(BF16)
        return carry

    lax.fori_loop(0, WIDE // 128, fill_scatter, 0)
    columns = lax.broadcasted_iota(jnp.int32, (128, 128), 1).astype(F32)
    for step in range(ROWS // 128):
        piece = slots[:, step * 128 : (step + 1) * 128].astype(F32)
        tall = jnp.broadcast_to(piece, (128, 128)).T
        for tile in range(WIDE // 128):
            gather[step * 128 : (step + 1) * 128, tile * 128 : (tile + 1) * 128] = (
                jnp.where(tall == columns + float(tile * 128), 1.0, 0.0).astype(BF16)
            )

    loads[3].wait()

    def split_rows(step, carry):
        rows = pl.ds(pl.multiple_of(step * 64, 64), 64)
        high[rows, :], low[rows, :] = split(full[rows, :])
        return carry

    lax.fori_loop(0, ROWS // 64, split_rows, 0)

    weight_low, weight_high = weights[0:1, part(0)], weights[0:1, part(1)]
    empty = jnp.zeros((MODES, SIDE), F32)
    moments_map[MODES : 2 * MODES, part(0)] = half_basis[0] * weight_low
    moments_map[MODES : 2 * MODES, part(1)] = half_basis[1] * weight_high
    for copy in basis_copies:
        copy.wait_recv()
    moments_map[0:MODES, part(0)] = -near_basis[0] * weight_low
    moments_map[0:MODES, part(1)] = empty
    moments_map[2 * MODES : 3 * MODES, part(0)] = empty
    moments_map[2 * MODES : 3 * MODES, part(1)] = -near_basis[1] * weight_high
    moments_map[3 * MODES : 4 * MODES, :] = jnp.zeros((MODES, PAIR), F32)

    def gather_start(buffer, value):
        buffer[core, z] = value
        return share(buffer.at[core], z, z_peers)

    def gather_finish(buffer, arrived):
        arrived.wait()
        return swap(buffer.at[core], buffer.at[core], (c, mate))

    def join_sides(target, halos, sides_out, copies):
        for copy in copies:
            copy.wait_recv()
        for side in range(4):
            target[:, part(side)] = sides_out[side] + halos[side]

    join_sides(first, halo_q, far_q, rhs_copies)
    q_moments = exact(moments_map[MODES : 2 * MODES, :], first[:, :PAIR], NT)
    q_arrived = gather_start(all_q, fold(q_moments))
    m_own = exact(moments_map[MODES : 2 * MODES, :], moments_map[...], NT)
    m_own = jnp.concatenate(
        [0.5 * m_own[:, MODES : 2 * MODES], m_own[:, 2 * MODES : 3 * MODES]], axis=1
    )
    m_arrived = gather_start(all_m, fold(m_own))

    map_high, map_low = split(moments_map[...] * weights[0:1, :PAIR])
    spread = single(jnp.concatenate([map_high, map_low], axis=0), scatter[:PAIR, :])
    map_high, map_low = split(spread[: 4 * MODES] + spread[4 * MODES :])
    moments_slots[: 4 * MODES] = map_high
    moments_slots[4 * MODES :] = map_low

    loads[2].wait()
    coarse[0:MODES, :] = jnp.zeros((MODES, COARSE), F32)
    coarse[MODES + COARSE :, :] = jnp.zeros((2 * MODES, COARSE), F32)
    near_rows = coarse[pl.ds(pl.multiple_of(s * MODES, MODES), 4 * MODES), :]
    mixed[:, 0:128] = near_rows.T
    dense_m[...] = jnp.zeros((COARSE, COARSE + 128), F32)

    q_crossed = gather_finish(all_q, q_arrived)
    m_crossed = gather_finish(all_m, m_arrived)
    m_crossed.wait_recv()
    lane = lax.broadcasted_iota(jnp.int32, (MODES, 128), 1)
    blank = jnp.zeros((MODES, 64), F32)
    for block in range(SUBS):
        tile, shift = block // 4, 32 * (block % 4)
        rows = slice(block * MODES, (block + 1) * MODES)
        value = jnp.concatenate([unfold(all_m[block % 2, block // 2]), blank], axis=1)
        if shift:
            value = pltpu.roll(value, shift, 1)
        if shift == 96:
            dense_m[rows, (tile + 1) * 128 : (tile + 2) * 128] = jnp.where(
                lane < shift, value, 0.0
            )
            value = jnp.where(lane >= shift, value, 0.0)
        dense_m[rows, tile * 128 : (tile + 1) * 128] = value
    square_m = dense_m[:, :COARSE]
    square_m = square_m + square_m.T
    inner = coarse[MODES : MODES + COARSE, :]
    mixed[:, 128:256] = (near_rows - exact(exact(near_rows, square_m), inner)).T
    for block in range(SUBS):
        to = ((block % 2) * 8 + block // 2) * 16
        table_even[to : to + 16, :] = mixed[block * MODES : block * MODES + 16, :]
        table_odd[to : to + 16, :] = mixed[block * MODES + 16 : (block + 1) * MODES, :]

    def coefficients(buffer):
        turned = buffer[...].reshape(SUBS * 16, 128).T
        return exact(turned[:COLS], table_even[...]) + exact(
            turned[COLS:], table_odd[...]
        )

    def place(which):
        return slice(which * COLS, (which + 1) * COLS)

    def project_pair(which, value_proj, factors, source):
        lift = exact(
            jnp.concatenate([factors[:, :128], factors[:, 128:]], axis=0),
            moments_map[...],
        )
        once = source[:, :PAIR] - lift[:COLS]
        basis[place(which), :PAIR] = once
        value_proj[:, :PAIR] = once - lift[COLS:]
        basis[place(which), PAIR:] = source[:, PAIR:]
        value_proj[:, PAIR:] = source[:, PAIR:]

    q_crossed.wait_recv()
    project_pair(0, proj, coefficients(all_q), first)

    def reduce_all(bufs, value):
        parts, along_x, along_y, along_z, halves = bufs
        rows = value.shape[0] // 2
        parts[0] = value[:rows]
        parts[1] = value[rows:]
        me = 2 * x + core
        along_x[me] = parts[core]
        slot = fresh()
        for peer in x_others[:1] + x_peers[:1] + x_others[1:3] + x_peers[1:] + x_others[3:]:
            theirs = parts.at[core if peer[1] is s else 1 - core]
            send(theirs, along_x.at[me], peer, slot)
        whole = along_x.at[pl.ds(0, 7)]
        pending.append(lambda: pltpu.make_async_copy(whole, whole, send_sem.at[slot]).wait())
        yield
        pltpu.make_async_copy(whole, whole, recv_sem.at[slot]).wait()
        along_y[y] = (
            ((along_x[0] + along_x[1]) + (along_x[2] + along_x[3]))
            + ((along_x[4] + along_x[5]) + (along_x[6] + along_x[7]))
        )
        arrived = share(along_y, y, y_peers)
        yield
        arrived.wait()
        along_z[z] = (along_y[0] + along_y[1]) + (along_y[2] + along_y[3])
        arrived = share(along_z, z, z_peers)
        yield
        arrived.wait()
        total = along_z[0]
        for i in range(1, 8):
            total = total + along_z[i]
        halves[core] = total
        copy = swap(halves.at[core], halves.at[core], (c, mate))
        yield
        copy.wait_recv()
        yield jnp.concatenate([halves[0], halves[1]], axis=0)

    def three_parts(value):
        high_v = value.astype(BF16)
        rest = value - high_v.astype(F32)
        return jnp.concatenate((high_v,) + split(rest), axis=0)

    def spread_slots(source):
        return single(three_parts(source[...] * weights[0:1, :]), scatter[...]).astype(BF16)

    def product(both):
        turned, small = single(both, high[...]), single(both[: 2 * COLS], low[...])
        return turned[:COLS] + (
            (turned[COLS : 2 * COLS] + small[:COLS])
            + (turned[2 * COLS :] + small[COLS:])
        )

    def energy(both, value):
        whole = both.astype(F32)
        whole = whole[:COLS] + (whole[COLS : 2 * COLS] + whole[2 * COLS :])
        return exact(whole, value, NT)

    def send_moments(parts, outs, nears):
        both = lax.dot_general(
            moments_slots[...], parts[: 2 * COLS], NT, preferred_element_type=F32
        )
        half = 4 * MODES
        shares = both[:half, :COLS] + both[half:, :COLS] + both[:half, COLS:]
        outs[0] = fold(shares[0:MODES])
        outs[1] = fold(shares[2 * MODES : 3 * MODES])
        copies = [
            swap(outs.at[0], nears.at[1], (c, down)),
            swap(outs.at[1], nears.at[0], (c, up)),
        ]
        return fold(shares[MODES : 2 * MODES]), copies

    def send_sides(parts, halos, sides_out):
        back = single(parts, gather[...])
        back = back[:COLS] + (back[COLS : 2 * COLS] + back[2 * COLS :])
        back = back * weights[0:1, :]
        copies = []
        for side in (2, 3, 0, 1):
            sides_out[side] = back[:, part(side)]
            copies.append(
                swap(sides_out.at[side], halos.at[FACING[side]], side_peers[side])
            )
        return copies

    def both_parts(value):
        return jnp.concatenate(split(value), axis=0)

    spread = spread_slots(proj)
    value = product(spread)
    parts = three_parts(value)
    own_part, near_copies = send_moments(parts, out_one, near_one)
    halo_copies = send_sides(parts, halo_one, far_one)
    curvature = energy(spread, value)
    start = basis[place(0), :]
    descent = 0.5 * exact(start, start, NT)
    reduction = reduce_all(sum_a, jnp.concatenate([curvature, descent], axis=1))
    next(reduction)
    for copy in near_copies:
        copy.wait_recv()
    arrived = gather_start(all_one, own_part + near_one[0] + near_one[1])
    join_sides(local, halo_one, far_one, halo_copies)
    next(reduction)
    crossed = gather_finish(all_one, arrived)
    next(reduction)
    crossed.wait_recv()
    project_pair(1, image_proj, coefficients(all_one), local)
    image = basis[place(1), :]
    second = reduce_all(sum_b, fold(0.5 * exact(image, image, NT)))
    next(second)

    spread = spread_slots(image_proj)
    value = product(spread)
    third = reduce_all(sum_c, fold(energy(spread, value)))
    next(third)
    next(second)
    next(reduction)
    parts = three_parts(value)
    own_part, near_copies = send_moments(parts, out_two, near_two)
    halo_copies = send_sides(parts, halo_two, far_two)
    both_grams = next(reduction)
    curvature, descent = both_grams[:, :COLS], both_grams[:, COLS:]
    next(third)
    next(second)
    for copy in near_copies:
        copy.wait_recv()
    arrived = gather_start(all_two, own_part + near_two[0] + near_two[1])
    row = lax.broadcasted_iota(jnp.int32, (COLS, COLS), 0)
    lane = lax.broadcasted_iota(jnp.int32, (COLS, COLS), 1)
    inverse = eliminate(curvature, jnp.where(row == lane, 1.0, 0.0))
    alpha, alpha_t = exact(inverse, descent), exact(descent, inverse)
    next(third)
    next(second)
    join_sides(local, halo_two, far_two, halo_copies)
    norm = unfold(next(second))
    moved = exact(norm, alpha)
    blend = exact(inverse, moved)
    known = exact(alpha_t, exact(norm, blend))
    descent_two = exact(alpha_t, moved) - descent
    crossed = gather_finish(all_two, arrived)
    next(third)
    crossed.wait_recv()
    factors = coefficients(all_two)
    lift = exact(factors[:, :128], moments_map[...])
    basis[place(2), :PAIR] = local[:, :PAIR] - lift
    basis[place(2), PAIR:] = local[:, PAIR:]
    cubic = unfold(next(third))

    curvature_two = exact(alpha_t, exact(cubic, alpha)) - known
    alpha_two = eliminate(curvature_two, descent_two)
    outer = (alpha + exact(blend, alpha_two)).T
    cross = exact(alpha, alpha_two).T
    none = jnp.zeros((COLS, COLS), F32)
    mix = jnp.concatenate(
        [
            jnp.concatenate([outer, -cross, none], axis=1),
            jnp.concatenate([none, -outer, cross], axis=1),
        ],
        axis=0,
    )
    for side in range(4):
        result = exact(mix, basis[:, part(side)])
        at = slice(side * FACE, (side + 1) * FACE)
        out_sol[:, at] = result[:COLS, :FACE]
        out_res[:, at] = (basis[place(0), part(side)] + result[COLS:])[:, :FACE]
    stores = [
        pltpu.make_async_copy(out_sol, sol_hbm.at[0, 0], local_sem.at[4]),
        pltpu.make_async_copy(out_res, res_hbm.at[0, 0], local_sem.at[5]),
    ]
    for store in stores:
        store.start()
    for wait in pending:
        wait()
    for store in stores:
        store.wait()


def shards(dual_ops, contributions, block_sizes, mult_map, coarse_basis, coarse_inverse):
    def vmem(*shape, dtype=F32):
        return pltpu.VMEM(shape, dtype)

    def sums(rows):
        return (
            vmem(2, rows, 128), vmem(8, rows, 128), vmem(4, rows, 128),
            vmem(8, rows, 128), vmem(2, rows, 128),
        )

    vector = vmem(COLS, WIDE)
    moments = vmem(2, 8, 16, 128)
    sides, pair = vmem(4, COLS, SIDE), vmem(2, 16, 128)
    anywhere = pl.BlockSpec(memory_space=pl.ANY)
    out = jax.ShapeDtypeStruct((1, 1, COLS, ROWS), F32)
    results = pl.pallas_call(
        kernel,
        out_shape=(out, out),
        in_specs=[
            anywhere, anywhere, pl.BlockSpec(memory_space=pltpu.SMEM),
            pl.BlockSpec(memory_space=pltpu.VMEM), anywhere, anywhere,
        ],
        out_specs=(anywhere, anywhere),
        scratch_shapes=[
            vmem(ROWS, ROWS), vmem(ROWS, ROWS, dtype=BF16), vmem(ROWS, ROWS, dtype=BF16),
            vmem(WIDE, ROWS, dtype=BF16), vmem(ROWS, WIDE, dtype=BF16),
            vmem(8 * MODES, ROWS, dtype=BF16),
            vmem(COLS, ROWS), sides, sides, vmem(MODES, 2 * FACE), vmem(2, MODES, SIDE),
            vmem(2, MODES, SIDE), vmem(COARSE + 3 * MODES, COARSE),
            vmem(4 * MODES, PAIR),
            vmem(8, WIDE), vector, vmem(3 * COLS, WIDE), vector, vector, vector,
            sides, sides, pair, pair, pair, pair, sides, sides,
            moments, moments, moments, moments,
            vmem(COARSE, 256), vmem(256, 256), vmem(256, 256), vmem(COARSE, COARSE + 128),
            sums(32), sums(16), sums(16), vmem(COLS, ROWS), vmem(COLS, ROWS),
            pltpu.SemaphoreType.DMA((6,)), pltpu.SemaphoreType.DMA((64,)),
            pltpu.SemaphoreType.DMA((64,)),
        ],
        compiler_params=pltpu.CompilerParams(
            collective_id=0, has_side_effects=True, vmem_limit_bytes=60 * 1024 * 1024
        ),
    )(
        dual_ops, jnp.swapaxes(contributions, 2, 3), block_sizes, mult_map,
        coarse_basis, coarse_inverse,
    )
    return tuple(jnp.swapaxes(result, 2, 3) for result in results)


def solution(mesh):
    return jax.shard_map(
        shards,
        mesh=mesh,
        in_specs=(
            P("cluster", "sub", None, None),
            P("cluster", "sub", None, None),
            P("cluster", "sub", None),
            P("cluster", "sub", None),
            P("cluster", "sub", None, None),
            P("cluster", None, None),
        ),
        out_specs=(P("cluster", "sub", None, None), P("cluster", "sub", None, None)),
        check_vma=False,
    )
```

```python
import jax
import jax.numpy as jnp
from jax import lax
from jax.sharding import PartitionSpec as P
from jax.experimental import pallas as pl
from jax.experimental.pallas import tpu as pltpu


ROWS = 1408
FACE = 352
SIDE = 384
WIDE = 4 * SIDE
PAIR = 2 * SIDE
COLS = 64
MODES = 32
SUBS = 16
COARSE = 512
SIGNS = (-1.0, 1.0, -1.0, 1.0)
FACING = (1, 0, 3, 2)

F32 = jnp.float32
BF16 = jnp.bfloat16
NN = (((1,), (0,)), ((), ()))
NT = (((1,), (1,)), ((), ()))


def exact(left, right, dims=NN):
    return lax.dot_general(
        left, right, dims, precision=lax.Precision.HIGHEST, preferred_element_type=F32
    )


def single(left, right):
    return lax.dot_general(left, right, NN, preferred_element_type=F32)


def split(value):
    high = value.astype(BF16)
    return high, (value - high.astype(F32)).astype(BF16)


def fold(value):
    half = value.shape[0] // 2
    return jnp.concatenate([value[:half], value[half:]], axis=1)


def unfold(value):
    half = value.shape[1] // 2
    return jnp.concatenate([value[:, :half], value[:, half:]], axis=0)


def part(side):
    return slice(side * SIDE, (side + 1) * SIDE)


def eliminate(left, right):
    joined = jnp.concatenate([left, right], axis=1)
    table = [joined[8 * r : 8 * r + 8] for r in range(8)]
    row = lax.broadcasted_iota(jnp.int32, (8, 2 * COLS), 0)
    for block in range(8):
        columns = [
            [
                jnp.broadcast_to(rows[:, 8 * block + j : 8 * block + j + 1], (8, 2 * COLS))
                for j in range(8)
            ]
            for rows in table
        ]
        panel, own = table[block], columns[block]
        for j in range(8):
            scale = 1.0 / own[j][j : j + 1]
            line = panel[j : j + 1] * scale
            panel = jnp.where(row == j, line, panel - own[j] * line)
            for k in range(j + 1, 8):
                entry = own[k][j : j + 1] * scale
                own[k] = jnp.where(row == j, entry, own[k] - own[j] * entry)
        for r in range(8):
            if r == block:
                table[r] = panel
            else:
                for j in range(8):
                    table[r] = table[r] - columns[r][j] * panel[j : j + 1]
    return jnp.concatenate(table, axis=0)[:, COLS:]


def kernel(
    ops_hbm, contrib_hbm, sizes_hbm, map_hbm, basis_hbm, coarse_hbm,
    sol_ref, res_ref,
    sizes, slot_map, full, high, low, scatter, gather, moments_slots,
    own_rhs, halo_q, far_q, own_basis, half_basis, near_basis, coarse, moments_map,
    weights, first, basis, proj, image_proj, local,
    halo_one, halo_two, near_one, near_two, out_one, out_two, far_one, far_two,
    all_q, all_m, all_one, all_two, mixed, table_even, table_odd, dense_m,
    sum_a, sum_b, sum_c,
    local_sem, send_sem, recv_sem,
):
    c, s = lax.axis_index("cluster"), lax.axis_index("sub")
    x, y = lax.div(c, 4), lax.rem(c, 4)
    z, core = lax.div(s, 2), lax.rem(s, 2)
    down, up = lax.rem(s + SUBS - 1, SUBS), lax.rem(s + 1, SUBS)
    west, east = lax.rem(c + 15, 16), lax.rem(c + 1, 16)
    mate = z * 2 + 1 - core
    x_peers = [(lax.rem(x + i, 4) * 4 + y, s) for i in (2, 1, 3)]
    x_others = [(lax.rem(x + i, 4) * 4 + y, mate) for i in (2, 1, 3, 0)]
    y_peers = [(x * 4 + lax.rem(y + i, 4), s) for i in (2, 1, 3)]
    z_peers = [(c, lax.rem(z + i, 8) * 2 + core) for i in (4, 3, 5, 2, 6, 1, 7)]
    side_peers = ((c, down), (c, up), (west, s), (east, s))
    used = [0]

    def fresh():
        used[0] += 1
        return used[0] - 1

    loads = [
        pltpu.make_async_copy(contrib_hbm.at[0, 0], own_rhs, local_sem.at[0]),
        pltpu.make_async_copy(basis_hbm.at[0, 0], own_basis, local_sem.at[1]),
        pltpu.make_async_copy(
            coarse_hbm.at[0], coarse.at[pl.ds(MODES, COARSE)], local_sem.at[2]
        ),
        pltpu.make_async_copy(ops_hbm.at[0, 0], full, local_sem.at[3]),
        pltpu.make_async_copy(map_hbm, slot_map, local_sem.at[6]),
        pltpu.make_async_copy(sizes_hbm, sizes, local_sem.at[7]),
    ]
    for load in loads[4:] + loads[:4]:
        load.start()

    barrier = pltpu.get_barrier_semaphore()
    greeted = z_peers + x_peers + x_others + y_peers
    greeted += [(c, down), (c, up), (west, s), (east, s)]
    for peer in greeted:
        pl.semaphore_signal(
            barrier, inc=1, device_id=peer, device_id_type=pl.DeviceIdType.MESH
        )

    loads[5].wait()
    lanes = lax.broadcasted_iota(jnp.int32, (8, SIDE), 1)
    for side in range(4):
        weights[:, part(side)] = jnp.where(lanes < sizes[0, 0, side], SIGNS[side], 0.0)
    loads[0].wait()
    zero_columns = jnp.zeros((COLS, SIDE - FACE), F32)
    for side in range(4):
        own = own_rhs[:, side * FACE : (side + 1) * FACE]
        far_q[side] = (
            jnp.concatenate([own, zero_columns], axis=1) * weights[0:1, part(side)]
        )
    loads[1].wait()
    zero_lanes = jnp.zeros((MODES, SIDE - FACE), F32)
    for side in range(2):
        own = own_basis[:, side * FACE : (side + 1) * FACE]
        half_basis[side] = jnp.concatenate([own, zero_lanes], axis=1)
    pl.semaphore_wait(barrier, len(greeted))

    def send(source, target, peer, slot):
        copy = pltpu.make_async_remote_copy(
            src_ref=source, dst_ref=target,
            send_sem=send_sem.at[slot], recv_sem=recv_sem.at[slot],
            device_id=peer, device_id_type=pl.DeviceIdType.MESH,
        )
        copy.start()
        return copy

    pending = []

    def share(buffer, me, peers):
        slot = fresh()
        for peer in peers:
            send(buffer.at[me], buffer.at[me], peer, slot)
        whole = buffer.at[pl.ds(0, len(peers))]
        pending.append(lambda: pltpu.make_async_copy(whole, whole, send_sem.at[slot]).wait())
        return pltpu.make_async_copy(whole, whole, recv_sem.at[slot])

    def swap(source, target, peer):
        copy = send(source, target, peer, fresh())
        pending.append(copy.wait_send)
        return copy

    basis_copies = [
        swap(half_basis.at[0], near_basis.at[1], (c, down)),
        swap(half_basis.at[1], near_basis.at[0], (c, up)),
    ]
    rhs_copies = [
        swap(far_q.at[side], halo_q.at[FACING[side]], side_peers[side])
        for side in (2, 3, 0, 1)
    ]

    loads[4].wait()
    slots = slot_map[0]
    slots = slots + (SIDE - FACE) * (
        (slots >= FACE).astype(jnp.int32)
        + (slots >= 2 * FACE).astype(jnp.int32)
        + (slots >= 3 * FACE).astype(jnp.int32)
    )

    def fill_scatter(step, carry):
        rows = pl.ds(pl.multiple_of(step * 128, 128), 128)
        index = lax.broadcasted_iota(jnp.int32, (128, ROWS), 0) + step * 128
        scatter[rows, :] = jnp.where(index == slots, 1.0, 0.0).astype(BF16)
        return carry

    lax.fori_loop(0, WIDE // 128, fill_scatter, 0)
    weight_low, weight_high = weights[0:1, part(0)], weights[0:1, part(1)]
    empty = jnp.zeros((MODES, SIDE), F32)
    moments_map[MODES : 2 * MODES, part(0)] = half_basis[0] * weight_low
    moments_map[MODES : 2 * MODES, part(1)] = half_basis[1] * weight_high
    for copy in basis_copies:
        copy.wait_recv()
    moments_map[0:MODES, part(0)] = -near_basis[0] * weight_low
    moments_map[0:MODES, part(1)] = empty
    moments_map[2 * MODES : 3 * MODES, part(0)] = empty
    moments_map[2 * MODES : 3 * MODES, part(1)] = -near_basis[1] * weight_high
    moments_map[3 * MODES : 4 * MODES, :] = jnp.zeros((MODES, PAIR), F32)

    def gather_start(buffer, value):
        buffer[core, z] = value
        return share(buffer.at[core], z, z_peers)

    def gather_finish(buffer, arrived):
        arrived.wait()
        return swap(buffer.at[core], buffer.at[core], (c, mate))

    m_own = exact(moments_map[MODES : 2 * MODES, :], moments_map[...], NT)
    m_own = jnp.concatenate(
        [0.5 * m_own[:, MODES : 2 * MODES], m_own[:, 2 * MODES : 3 * MODES]], axis=1
    )
    m_arrived = gather_start(all_m, fold(m_own))

    columns = lax.broadcasted_iota(jnp.int32, (128, 128), 1).astype(F32)
    for step in range(ROWS // 128):
        piece = slots[:, step * 128 : (step + 1) * 128].astype(F32)
        tall = jnp.broadcast_to(piece, (128, 128)).T
        for tile in range(WIDE // 128):
            gather[step * 128 : (step + 1) * 128, tile * 128 : (tile + 1) * 128] = (
                jnp.where(tall == columns + float(tile * 128), 1.0, 0.0).astype(BF16)
            )

    map_high, map_low = split(moments_map[...] * weights[0:1, :PAIR])
    spread = single(jnp.concatenate([map_high, map_low], axis=0), scatter[:PAIR, :])
    map_high, map_low = split(spread[: 4 * MODES] + spread[4 * MODES :])
    moments_slots[: 4 * MODES] = map_high
    moments_slots[4 * MODES :] = map_low

    def join_sides(target, halos, sides_out, copies):
        for copy in copies:
            copy.wait_recv()
        for side in range(4):
            target[:, part(side)] = sides_out[side] + halos[side]

    join_sides(first, halo_q, far_q, rhs_copies)
    q_moments = exact(moments_map[MODES : 2 * MODES, :], first[:, :PAIR], NT)
    q_arrived = gather_start(all_q, fold(q_moments))
    def split_rows(step, carry):
        rows = pl.ds(pl.multiple_of(step * 64, 64), 64)
        high[rows, :], low[rows, :] = split(full[rows, :])
        return carry

    m_crossed = gather_finish(all_m, m_arrived)
    loads[2].wait()
    coarse[0:MODES, :] = jnp.zeros((MODES, COARSE), F32)
    coarse[MODES + COARSE :, :] = jnp.zeros((2 * MODES, COARSE), F32)
    near_rows = coarse[pl.ds(pl.multiple_of(s * MODES, MODES), 4 * MODES), :]
    mixed[:, 0:128] = near_rows.T
    dense_m[...] = jnp.zeros((COARSE, COARSE + 128), F32)

    loads[3].wait()
    lax.fori_loop(0, ROWS // 128, split_rows, 0)
    m_crossed.wait_recv()
    lane = lax.broadcasted_iota(jnp.int32, (MODES, 128), 1)
    blank = jnp.zeros((MODES, 64), F32)
    for block in range(SUBS):
        tile, shift = block // 4, 32 * (block % 4)
        rows = slice(block * MODES, (block + 1) * MODES)
        value = jnp.concatenate([unfold(all_m[block % 2, block // 2]), blank], axis=1)
        if shift:
            value = pltpu.roll(value, shift, 1)
        if shift == 96:
            dense_m[rows, (tile + 1) * 128 : (tile + 2) * 128] = jnp.where(
                lane < shift, value, 0.0
            )
            value = jnp.where(lane >= shift, value, 0.0)
        dense_m[rows, tile * 128 : (tile + 1) * 128] = value
    square_m = dense_m[:, :COARSE]
    square_m = square_m + square_m.T
    inner = coarse[MODES : MODES + COARSE, :]
    mixed[:, 128:256] = (near_rows - exact(exact(near_rows, square_m), inner)).T
    for block in range(SUBS):
        to = ((block % 2) * 8 + block // 2) * 16
        table_even[to : to + 16, :] = mixed[block * MODES : block * MODES + 16, :]
        table_odd[to : to + 16, :] = mixed[block * MODES + 16 : (block + 1) * MODES, :]

    def coefficients(buffer):
        turned = buffer[...].reshape(SUBS * 16, 128).T
        return exact(turned[:COLS], table_even[...]) + exact(
            turned[COLS:], table_odd[...]
        )

    def place(which):
        return slice(which * COLS, (which + 1) * COLS)

    def project_pair(which, value_proj, factors, source):
        lift = exact(
            jnp.concatenate([factors[:, :128], factors[:, 128:]], axis=0),
            moments_map[...],
        )
        once = source[:, :PAIR] - lift[:COLS]
        basis[place(which), :PAIR] = once
        value_proj[:, :PAIR] = once - lift[COLS:]
        basis[place(which), PAIR:] = source[:, PAIR:]
        value_proj[:, PAIR:] = source[:, PAIR:]

    q_crossed = gather_finish(all_q, q_arrived)
    lax.fori_loop(ROWS // 128, ROWS // 64, split_rows, 0)
    q_crossed.wait_recv()
    project_pair(0, proj, coefficients(all_q), first)

    def reduce_all(bufs, value):
        parts, along_x, along_y, along_z, halves = bufs
        rows = value.shape[0] // 2
        parts[0] = value[:rows]
        parts[1] = value[rows:]
        me = 2 * x + core
        along_x[me] = parts[core]
        slot = fresh()
        for peer in x_others[:1] + x_peers[:1] + x_others[1:3] + x_peers[1:] + x_others[3:]:
            theirs = parts.at[core if peer[1] is s else 1 - core]
            send(theirs, along_x.at[me], peer, slot)
        whole = along_x.at[pl.ds(0, 7)]
        pending.append(lambda: pltpu.make_async_copy(whole, whole, send_sem.at[slot]).wait())
        yield
        pltpu.make_async_copy(whole, whole, recv_sem.at[slot]).wait()
        along_y[y] = (
            ((along_x[0] + along_x[1]) + (along_x[2] + along_x[3]))
            + ((along_x[4] + along_x[5]) + (along_x[6] + along_x[7]))
        )
        arrived = share(along_y, y, y_peers)
        yield
        arrived.wait()
        along_z[z] = (along_y[0] + along_y[1]) + (along_y[2] + along_y[3])
        arrived = share(along_z, z, z_peers)
        yield
        arrived.wait()
        total = along_z[0]
        for i in range(1, 8):
            total = total + along_z[i]
        halves[core] = total
        copy = swap(halves.at[core], halves.at[core], (c, mate))
        yield
        copy.wait_recv()
        yield jnp.concatenate([halves[0], halves[1]], axis=0)

    def three_parts(value):
        high_v = value.astype(BF16)
        rest = value - high_v.astype(F32)
        return jnp.concatenate((high_v,) + split(rest), axis=0)

    def spread_slots(source):
        return single(three_parts(source[...] * weights[0:1, :]), scatter[...]).astype(BF16)

    def product(both):
        turned, small = single(both, high[...]), single(both[: 2 * COLS], low[...])
        return turned[:COLS] + (
            (turned[COLS : 2 * COLS] + small[:COLS])
            + (turned[2 * COLS :] + small[COLS:])
        )

    def energy(both, value):
        whole = both.astype(F32)
        whole = whole[:COLS] + (whole[COLS : 2 * COLS] + whole[2 * COLS :])
        return exact(whole, value, NT)

    def send_moments(parts, outs, nears):
        both = lax.dot_general(
            moments_slots[...], parts[: 2 * COLS], NT, preferred_element_type=F32
        )
        half = 4 * MODES
        shares = both[:half, :COLS] + both[half:, :COLS] + both[:half, COLS:]
        outs[0] = fold(shares[0:MODES])
        outs[1] = fold(shares[2 * MODES : 3 * MODES])
        copies = [
            swap(outs.at[0], nears.at[1], (c, down)),
            swap(outs.at[1], nears.at[0], (c, up)),
        ]
        return fold(shares[MODES : 2 * MODES]), copies

    def send_sides(parts, halos, sides_out):
        back = single(parts, gather[...])
        back = back[:COLS] + (back[COLS : 2 * COLS] + back[2 * COLS :])
        back = back * weights[0:1, :]
        copies = []
        for side in (2, 3, 0, 1):
            sides_out[side] = back[:, part(side)]
            copies.append(
                swap(sides_out.at[side], halos.at[FACING[side]], side_peers[side])
            )
        return copies

    def both_parts(value):
        return jnp.concatenate(split(value), axis=0)

    spread = spread_slots(proj)
    value = product(spread)
    parts = three_parts(value)
    own_part, near_copies = send_moments(parts, out_one, near_one)
    halo_copies = send_sides(parts, halo_one, far_one)
    curvature = energy(spread, value)
    start = basis[place(0), :]
    descent = 0.5 * exact(start, start, NT)
    reduction = reduce_all(sum_a, jnp.concatenate([curvature, descent], axis=1))
    next(reduction)
    for copy in near_copies:
        copy.wait_recv()
    arrived = gather_start(all_one, own_part + near_one[0] + near_one[1])
    join_sides(local, halo_one, far_one, halo_copies)
    next(reduction)
    crossed = gather_finish(all_one, arrived)
    next(reduction)
    crossed.wait_recv()
    project_pair(1, image_proj, coefficients(all_one), local)
    image = basis[place(1), :]
    second = reduce_all(sum_b, fold(0.5 * exact(image, image, NT)))
    next(second)

    spread = spread_slots(image_proj)
    value = product(spread)
    third = reduce_all(sum_c, fold(energy(spread, value)))
    next(third)
    next(second)
    next(reduction)
    parts = three_parts(value)
    own_part, near_copies = send_moments(parts, out_two, near_two)
    halo_copies = send_sides(parts, halo_two, far_two)
    both_grams = next(reduction)
    curvature, descent = both_grams[:, :COLS], both_grams[:, COLS:]
    next(third)
    next(second)
    for copy in near_copies:
        copy.wait_recv()
    arrived = gather_start(all_two, own_part + near_two[0] + near_two[1])
    row = lax.broadcasted_iota(jnp.int32, (COLS, COLS), 0)
    lane = lax.broadcasted_iota(jnp.int32, (COLS, COLS), 1)
    inverse = eliminate(curvature, jnp.where(row == lane, 1.0, 0.0))
    alpha, alpha_t = exact(inverse, descent), exact(descent, inverse)
    next(third)
    next(second)
    join_sides(local, halo_two, far_two, halo_copies)
    norm = unfold(next(second))
    moved = exact(norm, alpha)
    blend = exact(inverse, moved)
    known = exact(alpha_t, exact(norm, blend))
    descent_two = exact(alpha_t, moved) - descent
    crossed = gather_finish(all_two, arrived)
    next(third)
    crossed.wait_recv()
    factors = coefficients(all_two)
    lift = exact(factors[:, :128], moments_map[...])
    basis[place(2), :PAIR] = local[:, :PAIR] - lift
    basis[place(2), PAIR:] = local[:, PAIR:]
    cubic = unfold(next(third))

    curvature_two = exact(alpha_t, exact(cubic, alpha)) - known
    alpha_two = eliminate(curvature_two, descent_two)
    both = exact(jnp.concatenate([blend, alpha], axis=0), alpha_two)
    outer, cross = (alpha + both[:COLS]).T, both[COLS:].T
    none = jnp.zeros((COLS, COLS), F32)
    mix = jnp.concatenate(
        [
            jnp.concatenate([outer, -cross, none], axis=1),
            jnp.concatenate([none, -outer, cross], axis=1),
        ],
        axis=0,
    )
    for side in range(4):
        result = exact(mix, basis[:, part(side)])
        at = slice(side * FACE, (side + 1) * FACE)
        sol_ref[0, 0, :, at] = result[:COLS, :FACE]
        res_ref[0, 0, :, at] = (basis[place(0), part(side)] + result[COLS:])[:, :FACE]
    for wait in pending:
        wait()


def store(sol_in, res_in, sol_out, res_out, sem):
    copies = [
        pltpu.make_async_copy(sol_in, sol_out, sem.at[0]),
        pltpu.make_async_copy(res_in, res_out, sem.at[1]),
    ]
    for copy in copies:
        copy.start()
    for copy in copies:
        copy.wait()


def shards(dual_ops, contributions, block_sizes, mult_map, coarse_basis, coarse_inverse):
    def vmem(*shape, dtype=F32):
        return pltpu.VMEM(shape, dtype)

    def sums(rows):
        return (
            vmem(2, rows, 128), vmem(8, rows, 128), vmem(4, rows, 128),
            vmem(8, rows, 128), vmem(2, rows, 128),
        )

    vector = vmem(COLS, WIDE)
    moments = vmem(2, 8, 16, 128)
    sides, pair = vmem(4, COLS, SIDE), vmem(2, 16, 128)
    anywhere = pl.BlockSpec(memory_space=pl.ANY)
    near_spec = pl.BlockSpec(memory_space=pltpu.VMEM)
    out = jax.ShapeDtypeStruct((1, 1, COLS, ROWS), F32)
    results = pl.pallas_call(
        kernel,
        out_shape=(out, out),
        in_specs=[
            anywhere, anywhere, anywhere, anywhere, anywhere, anywhere,
        ],
        out_specs=(near_spec, near_spec),
        scratch_shapes=[
            pltpu.SMEM((1, 1, 4), jnp.int32), vmem(1, 1, ROWS, dtype=jnp.int32),
            vmem(ROWS, ROWS), vmem(ROWS, ROWS, dtype=BF16), vmem(ROWS, ROWS, dtype=BF16),
            vmem(WIDE, ROWS, dtype=BF16), vmem(ROWS, WIDE, dtype=BF16),
            vmem(8 * MODES, ROWS, dtype=BF16),
            vmem(COLS, ROWS), sides, sides, vmem(MODES, 2 * FACE), vmem(2, MODES, SIDE),
            vmem(2, MODES, SIDE), vmem(COARSE + 3 * MODES, COARSE),
            vmem(4 * MODES, PAIR),
            vmem(8, WIDE), vector, vmem(3 * COLS, WIDE), vector, vector, vector,
            sides, sides, pair, pair, pair, pair, sides, sides,
            moments, moments, moments, moments,
            vmem(COARSE, 256), vmem(256, 256), vmem(256, 256), vmem(COARSE, COARSE + 128),
            sums(32), sums(16), sums(16),
            pltpu.SemaphoreType.DMA((8,)), pltpu.SemaphoreType.DMA((64,)),
            pltpu.SemaphoreType.DMA((64,)),
        ],
        compiler_params=pltpu.CompilerParams(
            collective_id=0, has_side_effects=True, vmem_limit_bytes=55_500_000
        ),
    )(
        dual_ops, jnp.swapaxes(contributions, 2, 3), block_sizes, mult_map,
        coarse_basis, coarse_inverse,
    )
    results = pl.pallas_call(
        store, out_shape=(out, out), in_specs=[near_spec, near_spec],
        out_specs=(anywhere, anywhere), scratch_shapes=[pltpu.SemaphoreType.DMA((2,))],
        compiler_params=pltpu.CompilerParams(vmem_limit_bytes=4 * 1024 * 1024),
    )(*results)
    return tuple(jnp.swapaxes(result, 2, 3) for result in results)


def solution(mesh):
    return jax.shard_map(
        shards,
        mesh=mesh,
        in_specs=(
            P("cluster", "sub", None, None),
            P("cluster", "sub", None, None),
            P("cluster", "sub", None),
            P("cluster", "sub", None),
            P("cluster", "sub", None, None),
            P("cluster", None, None),
        ),
        out_specs=(P("cluster", "sub", None, None), P("cluster", "sub", None, None)),
        check_vma=False,
    )
```

```python
import jax
import jax.numpy as jnp
from jax import lax
from jax.sharding import PartitionSpec as P
from jax.experimental import pallas as pl
from jax.experimental.pallas import tpu as pltpu


ROWS = 1408
FACE = 352
SIDE = 384
WIDE = 4 * SIDE
PAIR = 2 * SIDE
COLS = 64
MODES = 32
SUBS = 16
COARSE = 512
SIGNS = (-1.0, 1.0, -1.0, 1.0)
FACING = (1, 0, 3, 2)

F32 = jnp.float32
BF16 = jnp.bfloat16
NN = (((1,), (0,)), ((), ()))
NT = (((1,), (1,)), ((), ()))


def exact(left, right, dims=NN):
    return lax.dot_general(
        left, right, dims, precision=lax.Precision.HIGHEST, preferred_element_type=F32
    )


def single(left, right):
    return lax.dot_general(left, right, NN, preferred_element_type=F32)


def split(value):
    high = value.astype(BF16)
    return high, (value - high.astype(F32)).astype(BF16)


def fold(value):
    half = value.shape[0] // 2
    return jnp.concatenate([value[:half], value[half:]], axis=1)


def unfold(value):
    half = value.shape[1] // 2
    return jnp.concatenate([value[:, :half], value[:, half:]], axis=0)


def part(side):
    return slice(side * SIDE, (side + 1) * SIDE)


def eliminate(left, right):
    joined = jnp.concatenate([left, right], axis=1)
    table = [joined[8 * r : 8 * r + 8] for r in range(8)]
    row = lax.broadcasted_iota(jnp.int32, (8, 2 * COLS), 0)
    for block in range(8):
        columns = [
            [
                jnp.broadcast_to(rows[:, 8 * block + j : 8 * block + j + 1], (8, 2 * COLS))
                for j in range(8)
            ]
            for rows in table
        ]
        panel, own = table[block], columns[block]
        for j in range(8):
            scale = 1.0 / own[j][j : j + 1]
            line = panel[j : j + 1] * scale
            panel = jnp.where(row == j, line, panel - own[j] * line)
            for k in range(j + 1, 8):
                entry = own[k][j : j + 1] * scale
                own[k] = jnp.where(row == j, entry, own[k] - own[j] * entry)
        for r in range(8):
            if r == block:
                table[r] = panel
            else:
                for j in range(8):
                    table[r] = table[r] - columns[r][j] * panel[j : j + 1]
    return jnp.concatenate(table, axis=0)[:, COLS:]


def kernel(
    ops_hbm, contrib_hbm, sizes_hbm, map_hbm, basis_hbm, coarse_hbm,
    sol_hbm, res_hbm,
    sizes, slot_map, full, high, low, scatter, gather, moments_slots,
    own_rhs, halo_q, far_q, own_basis, half_basis, near_basis, coarse, moments_map,
    weights, first, basis, proj, image_proj, local,
    halo_one, halo_two, near_one, near_two, out_one, out_two, far_one, far_two,
    all_q, all_m, all_one, all_two, mixed, table_even, table_odd, dense_m,
    sum_a, sum_b, sum_c, out_sol, out_res,
    local_sem, send_sem, recv_sem,
):
    c, s = lax.axis_index("cluster"), lax.axis_index("sub")
    x, y = lax.div(c, 4), lax.rem(c, 4)
    z, core = lax.div(s, 2), lax.rem(s, 2)
    down, up = lax.rem(s + SUBS - 1, SUBS), lax.rem(s + 1, SUBS)
    west, east = lax.rem(c + 15, 16), lax.rem(c + 1, 16)
    mate = z * 2 + 1 - core
    x_peers = [(lax.rem(x + i, 4) * 4 + y, s) for i in (2, 1, 3)]
    x_others = [(lax.rem(x + i, 4) * 4 + y, mate) for i in (2, 1, 3, 0)]
    y_peers = [(x * 4 + lax.rem(y + i, 4), s) for i in (2, 1, 3)]
    z_peers = [(c, lax.rem(z + i, 8) * 2 + core) for i in (4, 3, 5, 2, 6, 1, 7)]
    side_peers = ((c, down), (c, up), (west, s), (east, s))
    used = [0]

    def fresh():
        used[0] += 1
        return used[0] - 1

    loads = [
        pltpu.make_async_copy(contrib_hbm.at[0, 0], own_rhs, local_sem.at[0]),
        pltpu.make_async_copy(basis_hbm.at[0, 0], own_basis, local_sem.at[1]),
        pltpu.make_async_copy(
            coarse_hbm.at[0], coarse.at[pl.ds(MODES, COARSE)], local_sem.at[2]
        ),
        pltpu.make_async_copy(ops_hbm.at[0, 0], full, local_sem.at[3]),
        pltpu.make_async_copy(map_hbm, slot_map, local_sem.at[6]),
        pltpu.make_async_copy(sizes_hbm, sizes, local_sem.at[7]),
    ]
    for load in loads[4:] + loads[:4]:
        load.start()

    barrier = pltpu.get_barrier_semaphore()
    greeted = z_peers + x_peers + x_others + y_peers
    greeted += [(c, down), (c, up), (west, s), (east, s)]
    for peer in greeted:
        pl.semaphore_signal(
            barrier, inc=1, device_id=peer, device_id_type=pl.DeviceIdType.MESH
        )

    loads[5].wait()
    lanes = lax.broadcasted_iota(jnp.int32, (8, SIDE), 1)
    for side in range(4):
        weights[:, part(side)] = jnp.where(lanes < sizes[0, 0, side], SIGNS[side], 0.0)
    loads[0].wait()
    zero_columns = jnp.zeros((COLS, SIDE - FACE), F32)
    for side in range(4):
        own = own_rhs[:, side * FACE : (side + 1) * FACE]
        far_q[side] = (
            jnp.concatenate([own, zero_columns], axis=1) * weights[0:1, part(side)]
        )
    loads[1].wait()
    zero_lanes = jnp.zeros((MODES, SIDE - FACE), F32)
    for side in range(2):
        own = own_basis[:, side * FACE : (side + 1) * FACE]
        half_basis[side] = jnp.concatenate([own, zero_lanes], axis=1)
    pl.semaphore_wait(barrier, len(greeted))

    def send(source, target, peer, slot):
        copy = pltpu.make_async_remote_copy(
            src_ref=source, dst_ref=target,
            send_sem=send_sem.at[slot], recv_sem=recv_sem.at[slot],
            device_id=peer, device_id_type=pl.DeviceIdType.MESH,
        )
        copy.start()
        return copy

    pending = []

    def share(buffer, me, peers):
        slot = fresh()
        for peer in peers:
            send(buffer.at[me], buffer.at[me], peer, slot)
        whole = buffer.at[pl.ds(0, len(peers))]
        pending.append(lambda: pltpu.make_async_copy(whole, whole, send_sem.at[slot]).wait())
        return pltpu.make_async_copy(whole, whole, recv_sem.at[slot])

    def swap(source, target, peer):
        copy = send(source, target, peer, fresh())
        pending.append(copy.wait_send)
        return copy

    basis_copies = [
        swap(half_basis.at[0], near_basis.at[1], (c, down)),
        swap(half_basis.at[1], near_basis.at[0], (c, up)),
    ]
    rhs_copies = [
        swap(far_q.at[side], halo_q.at[FACING[side]], side_peers[side])
        for side in (2, 3, 0, 1)
    ]

    loads[4].wait()
    slots = slot_map[0]
    slots = slots + (SIDE - FACE) * (
        (slots >= FACE).astype(jnp.int32)
        + (slots >= 2 * FACE).astype(jnp.int32)
        + (slots >= 3 * FACE).astype(jnp.int32)
    )

    def fill_scatter(step, carry):
        rows = pl.ds(pl.multiple_of(step * 128, 128), 128)
        index = lax.broadcasted_iota(jnp.int32, (128, ROWS), 0) + step * 128
        scatter[rows, :] = jnp.where(index == slots, 1.0, 0.0).astype(BF16)
        return carry

    lax.fori_loop(0, WIDE // 128, fill_scatter, 0)
    weight_low, weight_high = weights[0:1, part(0)], weights[0:1, part(1)]
    empty = jnp.zeros((MODES, SIDE), F32)
    moments_map[MODES : 2 * MODES, part(0)] = half_basis[0] * weight_low
    moments_map[MODES : 2 * MODES, part(1)] = half_basis[1] * weight_high
    for copy in basis_copies:
        copy.wait_recv()
    moments_map[0:MODES, part(0)] = -near_basis[0] * weight_low
    moments_map[0:MODES, part(1)] = empty
    moments_map[2 * MODES : 3 * MODES, part(0)] = empty
    moments_map[2 * MODES : 3 * MODES, part(1)] = -near_basis[1] * weight_high
    moments_map[3 * MODES : 4 * MODES, :] = jnp.zeros((MODES, PAIR), F32)

    def gather_start(buffer, value):
        buffer[core, z] = value
        return share(buffer.at[core], z, z_peers)

    def gather_finish(buffer, arrived):
        arrived.wait()
        return swap(buffer.at[core], buffer.at[core], (c, mate))

    m_own = exact(moments_map[MODES : 2 * MODES, :], moments_map[...], NT)
    m_own = jnp.concatenate(
        [0.5 * m_own[:, MODES : 2 * MODES], m_own[:, 2 * MODES : 3 * MODES]], axis=1
    )
    m_arrived = gather_start(all_m, fold(m_own))

    columns = lax.broadcasted_iota(jnp.int32, (128, 128), 1).astype(F32)
    for step in range(ROWS // 128):
        piece = slots[:, step * 128 : (step + 1) * 128].astype(F32)
        tall = jnp.broadcast_to(piece, (128, 128)).T
        for tile in range(WIDE // 128):
            gather[step * 128 : (step + 1) * 128, tile * 128 : (tile + 1) * 128] = (
                jnp.where(tall == columns + float(tile * 128), 1.0, 0.0).astype(BF16)
            )

    map_high, map_low = split(moments_map[...] * weights[0:1, :PAIR])
    spread = single(jnp.concatenate([map_high, map_low], axis=0), scatter[:PAIR, :])
    map_high, map_low = split(spread[: 4 * MODES] + spread[4 * MODES :])
    moments_slots[: 4 * MODES] = map_high
    moments_slots[4 * MODES :] = map_low

    def join_sides(target, halos, sides_out, copies):
        for copy in copies:
            copy.wait_recv()
        for side in range(4):
            target[:, part(side)] = sides_out[side] + halos[side]

    join_sides(first, halo_q, far_q, rhs_copies)
    q_moments = exact(moments_map[MODES : 2 * MODES, :], first[:, :PAIR], NT)
    q_arrived = gather_start(all_q, fold(q_moments))
    def split_rows(step, carry):
        rows = pl.ds(pl.multiple_of(step * 64, 64), 64)
        high[rows, :], low[rows, :] = split(full[rows, :])
        return carry

    m_crossed = gather_finish(all_m, m_arrived)
    loads[2].wait()
    coarse[0:MODES, :] = jnp.zeros((MODES, COARSE), F32)
    coarse[MODES + COARSE :, :] = jnp.zeros((2 * MODES, COARSE), F32)
    near_rows = coarse[pl.ds(pl.multiple_of(s * MODES, MODES), 4 * MODES), :]
    mixed[:, 0:128] = near_rows.T
    dense_m[...] = jnp.zeros((COARSE, COARSE + 128), F32)

    loads[3].wait()
    lax.fori_loop(0, ROWS // 128, split_rows, 0)
    m_crossed.wait_recv()
    lane = lax.broadcasted_iota(jnp.int32, (MODES, 128), 1)
    blank = jnp.zeros((MODES, 64), F32)
    for block in range(SUBS):
        tile, shift = block // 4, 32 * (block % 4)
        rows = slice(block * MODES, (block + 1) * MODES)
        value = jnp.concatenate([unfold(all_m[block % 2, block // 2]), blank], axis=1)
        if shift:
            value = pltpu.roll(value, shift, 1)
        if shift == 96:
            dense_m[rows, (tile + 1) * 128 : (tile + 2) * 128] = jnp.where(
                lane < shift, value, 0.0
            )
            value = jnp.where(lane >= shift, value, 0.0)
        dense_m[rows, tile * 128 : (tile + 1) * 128] = value
    square_m = dense_m[:, :COARSE]
    square_m = square_m + square_m.T
    inner = coarse[MODES : MODES + COARSE, :]
    mixed[:, 128:256] = (near_rows - exact(exact(near_rows, square_m), inner)).T
    for block in range(SUBS):
        to = ((block % 2) * 8 + block // 2) * 16
        table_even[to : to + 16, :] = mixed[block * MODES : block * MODES + 16, :]
        table_odd[to : to + 16, :] = mixed[block * MODES + 16 : (block + 1) * MODES, :]

    def coefficients(buffer):
        turned = buffer[...].reshape(SUBS * 16, 128).T
        return exact(turned[:COLS], table_even[...]) + exact(
            turned[COLS:], table_odd[...]
        )

    def place(which):
        return slice(which * COLS, (which + 1) * COLS)

    def project_pair(which, value_proj, factors, source):
        lift = exact(
            jnp.concatenate([factors[:, :128], factors[:, 128:]], axis=0),
            moments_map[...],
        )
        once = source[:, :PAIR] - lift[:COLS]
        basis[place(which), :PAIR] = once
        value_proj[:, :PAIR] = once - lift[COLS:]
        basis[place(which), PAIR:] = source[:, PAIR:]
        value_proj[:, PAIR:] = source[:, PAIR:]

    q_crossed = gather_finish(all_q, q_arrived)
    lax.fori_loop(ROWS // 128, ROWS // 64, split_rows, 0)
    q_crossed.wait_recv()
    project_pair(0, proj, coefficients(all_q), first)

    def reduce_all(bufs, value):
        parts, along_x, along_y, along_z, halves = bufs
        rows = value.shape[0] // 2
        parts[0] = value[:rows]
        parts[1] = value[rows:]
        me = 2 * x + core
        along_x[me] = parts[core]
        slot = fresh()
        for peer in x_others[:1] + x_peers[:1] + x_others[1:3] + x_peers[1:] + x_others[3:]:
            theirs = parts.at[core if peer[1] is s else 1 - core]
            send(theirs, along_x.at[me], peer, slot)
        whole = along_x.at[pl.ds(0, 7)]
        pending.append(lambda: pltpu.make_async_copy(whole, whole, send_sem.at[slot]).wait())
        yield
        pltpu.make_async_copy(whole, whole, recv_sem.at[slot]).wait()
        along_y[y] = (
            ((along_x[0] + along_x[1]) + (along_x[2] + along_x[3]))
            + ((along_x[4] + along_x[5]) + (along_x[6] + along_x[7]))
        )
        arrived = share(along_y, y, y_peers)
        yield
        arrived.wait()
        along_z[z] = (along_y[0] + along_y[1]) + (along_y[2] + along_y[3])
        arrived = share(along_z, z, z_peers)
        yield
        arrived.wait()
        total = along_z[0]
        for i in range(1, 8):
            total = total + along_z[i]
        halves[core] = total
        copy = swap(halves.at[core], halves.at[core], (c, mate))
        yield
        copy.wait_recv()
        yield jnp.concatenate([halves[0], halves[1]], axis=0)

    def three_parts(value):
        high_v = value.astype(BF16)
        rest = value - high_v.astype(F32)
        return jnp.concatenate((high_v,) + split(rest), axis=0)

    def spread_slots(source):
        return single(three_parts(source[...] * weights[0:1, :]), scatter[...]).astype(BF16)

    def product(both):
        turned, small = single(both, high[...]), single(both[: 2 * COLS], low[...])
        return turned[:COLS] + (
            (turned[COLS : 2 * COLS] + small[:COLS])
            + (turned[2 * COLS :] + small[COLS:])
        )

    def energy(both, value):
        whole = both.astype(F32)
        whole = whole[:COLS] + (whole[COLS : 2 * COLS] + whole[2 * COLS :])
        return exact(whole, value, NT)

    def send_moments(parts, outs, nears):
        both = lax.dot_general(
            moments_slots[...], parts[: 2 * COLS], NT, preferred_element_type=F32
        )
        half = 4 * MODES
        shares = both[:half, :COLS] + both[half:, :COLS] + both[:half, COLS:]
        outs[0] = fold(shares[0:MODES])
        outs[1] = fold(shares[2 * MODES : 3 * MODES])
        copies = [
            swap(outs.at[0], nears.at[1], (c, down)),
            swap(outs.at[1], nears.at[0], (c, up)),
        ]
        return fold(shares[MODES : 2 * MODES]), copies

    def send_sides(parts, halos, sides_out):
        back = single(parts, gather[...])
        back = back[:COLS] + (back[COLS : 2 * COLS] + back[2 * COLS :])
        back = back * weights[0:1, :]
        copies = []
        for side in (2, 3, 0, 1):
            sides_out[side] = back[:, part(side)]
            copies.append(
                swap(sides_out.at[side], halos.at[FACING[side]], side_peers[side])
            )
        return copies

    def both_parts(value):
        return jnp.concatenate(split(value), axis=0)

    spread = spread_slots(proj)
    value = product(spread)
    parts = three_parts(value)
    own_part, near_copies = send_moments(parts, out_one, near_one)
    halo_copies = send_sides(parts, halo_one, far_one)
    curvature = energy(spread, value)
    start = basis[place(0), :]
    descent = 0.5 * exact(start, start, NT)
    reduction = reduce_all(sum_a, jnp.concatenate([curvature, descent], axis=1))
    next(reduction)
    for copy in near_copies:
        copy.wait_recv()
    arrived = gather_start(all_one, own_part + near_one[0] + near_one[1])
    join_sides(local, halo_one, far_one, halo_copies)
    next(reduction)
    crossed = gather_finish(all_one, arrived)
    next(reduction)
    crossed.wait_recv()
    project_pair(1, image_proj, coefficients(all_one), local)
    image = basis[place(1), :]
    second = reduce_all(sum_b, fold(0.5 * exact(image, image, NT)))
    next(second)

    spread = spread_slots(image_proj)
    value = product(spread)
    third = reduce_all(sum_c, fold(energy(spread, value)))
    next(third)
    next(second)
    next(reduction)
    parts = three_parts(value)
    own_part, near_copies = send_moments(parts, out_two, near_two)
    halo_copies = send_sides(parts, halo_two, far_two)
    both_grams = next(reduction)
    curvature, descent = both_grams[:, :COLS], both_grams[:, COLS:]
    next(third)
    next(second)
    for copy in near_copies:
        copy.wait_recv()
    arrived = gather_start(all_two, own_part + near_two[0] + near_two[1])
    row = lax.broadcasted_iota(jnp.int32, (COLS, COLS), 0)
    lane = lax.broadcasted_iota(jnp.int32, (COLS, COLS), 1)
    inverse = eliminate(curvature, jnp.where(row == lane, 1.0, 0.0))
    alpha, alpha_t = exact(inverse, descent), exact(descent, inverse)
    next(third)
    next(second)
    join_sides(local, halo_two, far_two, halo_copies)
    norm = unfold(next(second))
    moved = exact(norm, alpha)
    blend = exact(inverse, moved)
    known = exact(alpha_t, exact(norm, blend))
    descent_two = exact(alpha_t, moved) - descent
    crossed = gather_finish(all_two, arrived)
    next(third)
    crossed.wait_recv()
    factors = coefficients(all_two)
    lift = exact(factors[:, :128], moments_map[...])
    basis[place(2), :PAIR] = local[:, :PAIR] - lift
    basis[place(2), PAIR:] = local[:, PAIR:]
    cubic = unfold(next(third))

    curvature_two = exact(alpha_t, exact(cubic, alpha)) - known
    alpha_two = eliminate(curvature_two, descent_two)
    both = exact(jnp.concatenate([blend, alpha], axis=0), alpha_two)
    outer, cross = (alpha + both[:COLS]).T, both[COLS:].T
    none = jnp.zeros((COLS, COLS), F32)
    mix = jnp.concatenate(
        [
            jnp.concatenate([outer, -cross, none], axis=1),
            jnp.concatenate([none, -outer, cross], axis=1),
        ],
        axis=0,
    )
    for side in range(4):
        result = exact(mix, basis[:, part(side)])
        at = slice(side * FACE, (side + 1) * FACE)
        out_sol[:, at] = result[:COLS, :FACE]
        out_res[:, at] = (basis[place(0), part(side)] + result[COLS:])[:, :FACE]
    stores = [
        pltpu.make_async_copy(out_sol, sol_hbm.at[0, 0], local_sem.at[4]),
        pltpu.make_async_copy(out_res, res_hbm.at[0, 0], local_sem.at[5]),
    ]
    for store in stores:
        store.start()
    for wait in pending:
        wait()
    for store in stores:
        store.wait()


def store(sol_in, res_in, sol_out, res_out, held, in_sem, out_sem):
    loads, stores = [], []
    for which, (source, target) in enumerate(((sol_in, sol_out), (res_in, res_out))):
        for quarter in range(4):
            at, slot = pl.ds(16 * quarter, 16), 4 * which + quarter
            loads.append(
                pltpu.make_async_copy(
                    source.at[0, 0, at], held.at[which, at], in_sem.at[slot]
                )
            )
            stores.append(
                pltpu.make_async_copy(
                    held.at[which, at], target.at[0, 0, at], out_sem.at[slot]
                )
            )
    for load in loads:
        load.start()
    for load, copy in zip(loads, stores):
        load.wait()
        copy.start()
    for copy in stores:
        copy.wait()


def shards(dual_ops, contributions, block_sizes, mult_map, coarse_basis, coarse_inverse):
    def vmem(*shape, dtype=F32):
        return pltpu.VMEM(shape, dtype)

    def sums(rows):
        return (
            vmem(2, rows, 128), vmem(8, rows, 128), vmem(4, rows, 128),
            vmem(8, rows, 128), vmem(2, rows, 128),
        )

    vector = vmem(COLS, WIDE)
    moments = vmem(2, 8, 16, 128)
    sides, pair = vmem(4, COLS, SIDE), vmem(2, 16, 128)
    anywhere = pl.BlockSpec(memory_space=pl.ANY)
    out = jax.ShapeDtypeStruct((1, 1, COLS, ROWS), F32)
    results = pl.pallas_call(
        kernel,
        out_shape=(out, out),
        in_specs=[
            anywhere, anywhere, anywhere, anywhere, anywhere, anywhere,
        ],
        out_specs=(anywhere, anywhere),
        scratch_shapes=[
            pltpu.SMEM((1, 1, 4), jnp.int32), vmem(1, 1, ROWS, dtype=jnp.int32),
            vmem(ROWS, ROWS), vmem(ROWS, ROWS, dtype=BF16), vmem(ROWS, ROWS, dtype=BF16),
            vmem(WIDE, ROWS, dtype=BF16), vmem(ROWS, WIDE, dtype=BF16),
            vmem(8 * MODES, ROWS, dtype=BF16),
            vmem(COLS, ROWS), sides, sides, vmem(MODES, 2 * FACE), vmem(2, MODES, SIDE),
            vmem(2, MODES, SIDE), vmem(COARSE + 3 * MODES, COARSE),
            vmem(4 * MODES, PAIR),
            vmem(8, WIDE), vector, vmem(3 * COLS, WIDE), vector, vector, vector,
            sides, sides, pair, pair, pair, pair, sides, sides,
            moments, moments, moments, moments,
            vmem(COARSE, 256), vmem(256, 256), vmem(256, 256), vmem(COARSE, COARSE + 128),
            sums(32), sums(16), sums(16), vmem(COLS, ROWS), vmem(COLS, ROWS),
            pltpu.SemaphoreType.DMA((8,)), pltpu.SemaphoreType.DMA((64,)),
            pltpu.SemaphoreType.DMA((64,)),
        ],
        compiler_params=pltpu.CompilerParams(
            collective_id=0, has_side_effects=True, vmem_limit_bytes=60 * 1024 * 1024
        ),
    )(
        dual_ops, jnp.swapaxes(contributions, 2, 3), block_sizes, mult_map,
        coarse_basis, coarse_inverse,
    )
    results = pl.pallas_call(
        store, out_shape=(out, out), in_specs=[anywhere, anywhere],
        out_specs=(anywhere, anywhere),
        scratch_shapes=[
            vmem(2, COLS, ROWS), pltpu.SemaphoreType.DMA((8,)), pltpu.SemaphoreType.DMA((8,)),
        ],
        compiler_params=pltpu.CompilerParams(vmem_limit_bytes=60 * 1024 * 1024),
    )(*results)
    return tuple(jnp.swapaxes(result, 2, 3) for result in results)


def solution(mesh):
    return jax.shard_map(
        shards,
        mesh=mesh,
        in_specs=(
            P("cluster", "sub", None, None),
            P("cluster", "sub", None, None),
            P("cluster", "sub", None),
            P("cluster", "sub", None),
            P("cluster", "sub", None, None),
            P("cluster", None, None),
        ),
        out_specs=(P("cluster", "sub", None, None), P("cluster", "sub", None, None)),
        check_vma=False,
    )
```
